128 devices in a mesh: tm: 32 (over y, z, x_hi), head: 4 (over x_lo, core).
Axes of the slice: x: 4 (x_hi: 2, x_lo: 2; x = x_hi * 2 + x_lo), y: 4, z: 4, core: 2. Of those that a mesh axis runs over, the one named last changes fastest.
Arguments:
- query: bfloat16 [4096, 2560], P('tm', 'head'), may hold values from -8 to 8
- key: bfloat16 [4096, 2560], P('tm', 'head'), may hold values from -8 to 8
- value: bfloat16 [4096, 2560], P('tm', 'head'), may hold values from -6 to 6
- grad_out: bfloat16 [4096, 2560], P('tm', 'head'), may hold values from -6 to 6
- frame_ids: int32 [32], replicated, may hold values from 0 to 8, as said below
- sink_frame: int32 [1], replicated, may hold values from 0 to 8
- window: int32 [20], P('head'), may hold values from 1 to 3, as said below
Outputs:
- attended: bfloat16 [4096, 2560], P('tm', 'head')
- query_grad: bfloat16 [4096, 2560], P('tm', 'head')
- key_grad: bfloat16 [4096, 2560], P('tm', 'head')
- value_grad: bfloat16 [4096, 2560], P('tm', 'head')
The draws below stay inside these ranges and needn't reach their ends.
Inputs may be any that keep to these rules, and one draw needn't show every extreme that they name: frame_ids[b] = (b + c) // 4 for one c of 1 to 3: every frame is four blocks except the first and the last, which have 4 - c and c blocks. Some head has a window of 3 and some a window of 1.
All inputs are finite; a program needn't handle non-finite values.
Results may differ from the reference program's by a relative error of at most 0.033.
Values may be sent and summed in bfloat16 or wider, within the bound.
A program may use at most 128 MiB of HBM per device.

```python
import math
import jax
import jax.numpy as jnp
from jax import lax

HEADS = 20
DH = 128
NBLK = 32
TOKENS = 4096


def base_field(key, salt):
    inner = jax.random.fold_in(key, salt)
    return jnp.clip(jax.random.normal(inner, (TOKENS, HEADS * DH), jnp.float32), -6.0, 6.0)


def draw_query(key, part):
    field = base_field(key, 11)
    return field.astype(jnp.bfloat16)


def draw_key(key, part):
    field = base_field(key, 12)
    return field.astype(jnp.bfloat16)


def draw_frame_ids(key, part):
    start = jax.random.randint(jax.random.fold_in(key, 21), (), 1, 4)
    return ((jnp.arange(NBLK, dtype=jnp.int32) + start) // 4).astype(jnp.int32)


def draw_window(key, part):
    spans = jax.random.randint(jax.random.fold_in(key, 31), (HEADS,), 1, 4)
    order = jax.random.permutation(jax.random.fold_in(key, 32), HEADS)
    spans = spans.at[order[0]].set(3)
    spans = spans.at[order[1]].set(1)
    return spans.astype(jnp.int32)


def steps_of(own_key, extent, pieces, smallest, top_value):
    level, own = 1.0, jax.random.fold_in(own_key, 6)
    for axis_at, shards_of in pieces:
        heights = jnp.exp(jax.random.uniform(jax.random.fold_in(own, axis_at), (shards_of,), jnp.float32, smallest / len(pieces), top_value / len(pieces)))
        level = level * jnp.repeat(heights, extent[axis_at] // shards_of).reshape([-1 if axis == axis_at else 1 for axis in range(len(extent))])
    return level


def gaussian(own_key, dims, scale, most, cuts=(), held_as=jnp.bfloat16):
    result = scale * jax.random.normal(own_key, dims, jnp.float32)
    if cuts:
        result = result * steps_of(own_key, dims, cuts, -0.22, 0.18)
    return jnp.clip(result, -most, most).astype(held_as)


def setup_inputs(seed: int = 0) -> dict:
    keys = jax.random.split(jax.random.key(seed), 8)
    return {
        "query": draw_query(jax.random.fold_in(keys[7], 71), 0),
        "key": draw_key(jax.random.fold_in(keys[7], 71), 0),
        "value": gaussian(keys[2], (TOKENS, HEADS * DH), 1.0, 6.0, ((0, 32), (1, 4))),
        "grad_out": gaussian(keys[3], (TOKENS, HEADS * DH), 1.0, 6.0, ((0, 32), (1, 4))),
        "frame_ids": draw_frame_ids(jax.random.fold_in(keys[7], 71), 0),
        "sink_frame": jax.random.randint(keys[5], (1,), 0, NBLK // 4 + 1).astype(jnp.int32),
        "window": draw_window(jax.random.fold_in(keys[7], 71), 0),
    }


masked_score = -1e+30

def to_bf16_values(array):
    return lax.optimization_barrier(array.astype(jnp.bfloat16)).astype(jnp.float32)

def reference(query, key, value, grad_out, frame_ids, sink_frame, window):
    tokens, row_width = query.shape
    head_count = window.shape[0]
    head_dim = row_width // head_count
    blocks = frame_ids.shape[0]
    block_rows = tokens // blocks
    scaling = 1.0 / math.sqrt(head_dim)
    sink_index = sink_frame[0]
    query_heads = query.astype(jnp.float32).reshape(tokens, head_count, head_dim)
    key_heads = key.astype(jnp.float32).reshape(tokens, head_count, head_dim)
    value_heads = value.astype(jnp.float32).reshape(tokens, head_count, head_dim)
    grad_heads = grad_out.astype(jnp.float32).reshape(tokens, head_count, head_dim)
    key_frames = jnp.repeat(frame_ids, block_rows)

    def one_block(carry, block_id):
        key_acc, value_acc = carry
        query_frame = frame_ids[block_id]
        in_window = (key_frames[None, :] <= query_frame) & (key_frames[None, :] > query_frame - window[:, None])
        at_sink = (key_frames[None, :] == sink_index) & (sink_index <= query_frame)
        visible = (in_window | at_sink)[:, None, :]
        start = block_id * block_rows
        q_rows = lax.dynamic_slice_in_dim(query_heads, start, block_rows, 0)
        g_rows = lax.dynamic_slice_in_dim(grad_heads, start, block_rows, 0)
        scores = jnp.einsum('qhd,khd->hqk', q_rows, key_heads) * scaling
        scores = jnp.where(visible, scores, masked_score)
        top = lax.optimization_barrier(jnp.max(scores, axis=-1, keepdims=True))
        weights = jnp.where(visible, jnp.exp(scores - top), 0.0)
        totals = lax.optimization_barrier(jnp.sum(weights, axis=-1, keepdims=True))
        mixed = jnp.einsum('hqk,khd->hqd', to_bf16_values(weights), value_heads) / totals
        attended = mixed.transpose(1, 0, 2).astype(jnp.bfloat16)
        log_total = top + jnp.log(totals)
        probs_back = jnp.where(visible, jnp.exp(scores - log_total), 0.0)
        dot_back = jnp.einsum('qhd,khd->hqk', g_rows, value_heads)
        row_dots = lax.optimization_barrier(jnp.sum(g_rows * attended.astype(jnp.float32), axis=-1)).T[:, :, None]
        score_grad = to_bf16_values(probs_back * (dot_back - row_dots))
        query_grad = (jnp.einsum('hqk,khd->qhd', score_grad, key_heads) * scaling).astype(jnp.bfloat16)
        key_acc = key_acc + jnp.einsum('hqk,qhd->khd', score_grad, q_rows) * scaling
        value_acc = value_acc + jnp.einsum('hqk,qhd->khd', to_bf16_values(probs_back), g_rows)
        return ((key_acc, value_acc), (attended, query_grad))
    start_acc = jnp.zeros((tokens, head_count, head_dim), jnp.float32)
    (key_acc, value_acc), (attended, query_grad) = lax.scan(one_block, (start_acc, start_acc), jnp.arange(blocks, dtype=jnp.int32))
    attended = attended.reshape(tokens, row_width)
    query_grad = query_grad.reshape(tokens, row_width)
    key_grad = key_acc.reshape(tokens, row_width).astype(jnp.bfloat16)
    value_grad = value_acc.reshape(tokens, row_width).astype(jnp.bfloat16)
    return (attended, query_grad, key_grad, value_grad)
```

```python
import math

import jax
import jax.numpy as jnp
from jax import lax
from jax.experimental import pallas as pl
from jax.experimental.pallas import tpu as pltpu
from jax.sharding import PartitionSpec as P

MESH = pl.DeviceIdType.MESH
BLK = 128
DH = 128
HPD = 5
RING = 4
PLANE = 8
NBLK = RING * PLANE
BF16 = jnp.bfloat16
F32 = jnp.float32
TILE_Q = 2 * BLK
MAX_CHUNKS = 5
NEG = -1e30


def position():
    tm = lax.axis_index("tm")
    head = lax.axis_index("head")
    return tm // PLANE, tm % PLANE, head // 2, head % 2


def owner_of(j, x_lo, core):
    first = (2 * (j % 4) + j // 4, 0)
    u = HPD + j
    second = (2 * (u % 4) + u // 4, 0) if u < 8 else ((0, 5)[u - 8], 1)
    place = first[0] + core * (second[0] - first[0])
    core_there = first[1] + core * (second[1] - first[1])
    return place, 2 * (1 - x_lo) + core_there


def my_task(place, x_lo, core):
    u_first = (place % 2) * 4 + place // 2
    u = (1 - core) * u_first + core * (8 + place // 5)
    is_owner = (core == 0) | (place == 0) | (place == 5)
    return is_owner, 2 * (1 - x_lo) + u // HPD, u % HPD


def gather_kernel(
    q_ref, k_ref, v_ref, do_ref, w_ref,
    qo_ref, doo_ref, kvo_ref, wo_ref,
    send_sem, w_send, qd_sem, kv_sem, w_sem, up_sem, down_sem, up2_sem, down2_sem, ring_send,
):
    y, place, x_lo, core = position()
    is_owner, src_head, _ = my_task(place, x_lo, core)
    me_head = lax.axis_index("head")
    up = lax.rem(y + 1, RING)
    down = lax.rem(y + RING - 1, RING)
    far = lax.rem(y + 2, RING)
    base = y * PLANE
    up_id = (up * PLANE + place, me_head)
    down_id = (down * PLANE + place, me_head)

    barrier = pltpu.get_barrier_semaphore()

    @pl.when(is_owner)
    def _():
        for r in range(PLANE):
            pl.semaphore_signal(
                barrier, inc=1, device_id=(base + r, src_head), device_id_type=MESH
            )
        pl.semaphore_signal(barrier, inc=1, device_id=up_id, device_id_type=MESH)
        pl.semaphore_signal(barrier, inc=1, device_id=down_id, device_id_type=MESH)
        pl.semaphore_wait(barrier, HPD + 2)

    @pl.when(jnp.logical_not(is_owner))
    def _():
        pl.semaphore_wait(barrier, HPD)

    def column(ref, j):
        return ref.at[:, pl.ds(j * DH, DH)]

    rows = pl.ds(pl.multiple_of(place * BLK, BLK), BLK)
    owners = [owner_of(j, x_lo, core) for j in range(HPD)]
    targets = [(base + there, head) for there, head in owners]
    for j in range(HPD):
        for part, ref in enumerate((k_ref, v_ref)):
            pltpu.make_async_remote_copy(
                src_ref=column(ref, j), dst_ref=kvo_ref.at[base + place, part],
                send_sem=send_sem.at[part], recv_sem=kv_sem.at[place],
                device_id=targets[j], device_id_type=MESH,
            ).start()
    for j in range(HPD):
        for part, (ref, out) in enumerate(((q_ref, qo_ref), (do_ref, doo_ref))):
            pltpu.make_async_remote_copy(
                src_ref=column(ref, j), dst_ref=out.at[rows],
                send_sem=send_sem.at[2 + part], recv_sem=qd_sem.at[part],
                device_id=targets[j], device_id_type=MESH,
            ).start()

    @pl.when(place == 0)
    def _():
        for j in range(HPD):
            pltpu.make_async_remote_copy(
                src_ref=w_ref.at[j], dst_ref=wo_ref, send_sem=w_send, recv_sem=w_sem,
                device_id=targets[j], device_id_type=MESH,
            ).start()

    @pl.when(is_owner)
    def _():
        def pass_on(block, to, recv, lane):
            pltpu.make_async_remote_copy(
                src_ref=kvo_ref.at[block], dst_ref=kvo_ref.at[block],
                send_sem=ring_send.at[lane], recv_sem=recv,
                device_id=to, device_id_type=MESH,
            ).start()

        def arrived(block, sem):
            pltpu.make_async_copy(kvo_ref.at[block], kvo_ref.at[block], sem).wait()

        for r in range(PLANE):
            arrived(base + r, kv_sem.at[r])
            pass_on(base + r, up_id, up_sem.at[r], 0)
            pass_on(base + r, down_id, down_sem.at[r], 1)
        half = PLANE // 2
        for r in range(half):
            arrived(down * PLANE + r, up_sem.at[r])
            pass_on(down * PLANE + r, up_id, up2_sem.at[r], 2)
            arrived(up * PLANE + half + r, down_sem.at[half + r])
            pass_on(up * PLANE + half + r, down_id, down2_sem.at[r], 3)
        for r in range(half):
            arrived(down * PLANE + half + r, up_sem.at[half + r])
            arrived(up * PLANE + r, down_sem.at[r])
        for r in range(half):
            arrived(far * PLANE + r, up2_sem.at[r])
            arrived(far * PLANE + half + r, down2_sem.at[r])
        pltpu.make_async_copy(qo_ref, qo_ref, qd_sem.at[0]).wait()
        pltpu.make_async_copy(doo_ref, doo_ref, qd_sem.at[1]).wait()
        pltpu.make_async_copy(wo_ref, wo_ref, w_sem).wait()
        for lane, count in enumerate((PLANE, PLANE, half, half)):
            some = kvo_ref.at[pl.ds(0, count)]
            pltpu.make_async_copy(some, some, ring_send.at[lane]).wait()

    for part, ref in enumerate((k_ref, v_ref, q_ref, do_ref)):
        pltpu.make_async_copy(ref, ref, send_sem.at[part]).wait()

    @pl.when(place == 0)
    def _():
        pltpu.make_async_copy(w_ref, w_ref, w_send).wait()


def attend_kernel(
    fid_ref, sink_ref, w_ref, q_ref, do_ref, kv_ref,
    att_ref, dq_ref, dkv_ref,
    t_s, p_s, dk_s, dv_s,
):
    y, place, x_lo, core = position()
    is_owner, _, _ = my_task(place, x_lo, core)
    scale = 1.0 / math.sqrt(DH)
    slope = scale * math.log2(math.e)
    chunk = 4 * BLK

    @pl.when(is_owner)
    def _():
        c = 1 + fid_ref[1] + fid_ref[2]
        sink = sink_ref[0]
        win = w_ref[0, 0]
        dk_s[...] = jnp.zeros_like(dk_s)
        dv_s[...] = jnp.zeros_like(dv_s)
        lane = lax.broadcasted_iota(jnp.int32, (1, TILE_Q), 1)

        def sees(query_frame, frame):
            near = (frame <= query_frame) & (frame > query_frame - win)
            return near | ((frame == sink) & (sink <= query_frame))

        @pl.loop(0, PLANE // 2)
        def _(t):
            rows = pl.ds(pl.multiple_of(t * TILE_Q, TILE_Q), TILE_Q)
            block_a = y * PLANE + 2 * t
            frame_a = (block_a + c) // 4
            frame_b = (block_a + 1 + c) // 4
            low = jnp.maximum(frame_a - win + 1, 0)
            near_count = frame_b - low + 1
            count = near_count + (sink < low).astype(jnp.int32)

            def frame_at(i):
                return jnp.where(i < near_count, low + i, sink)

            def start_of(frame):
                return jnp.clip(4 * frame - c, 0, NBLK - 4)

            q_tile = q_ref[rows]
            q_t = q_tile.T

            def scores(i, top):
                frame = frame_at(i)
                start = start_of(frame)
                see_a = sees(frame_a, frame)
                see_b = sees(frame_b, frame)
                keys = kv_ref[pl.ds(start, 4), 0].reshape(chunk, DH)
                s = jnp.dot(keys, q_t, preferred_element_type=F32)
                for k in range(4):
                    here = (start + k + c) // 4 == frame
                    bias = jnp.where(
                        lane < BLK,
                        jnp.where(here & see_a, 0.0, NEG),
                        jnp.where(here & see_b, 0.0, NEG),
                    )
                    part = s[k * BLK : (k + 1) * BLK] + bias
                    t_s[pl.ds(i * chunk + k * BLK, BLK), :] = part
                    top = jnp.maximum(top, jnp.max(part.reshape(BLK // 8, 8, TILE_Q), axis=0))
                return top

            top = lax.fori_loop(0, count, scores, jnp.full((8, TILE_Q), NEG, F32))
            top = jnp.max(top, axis=0, keepdims=True) * slope

            def mix(i, carry):
                total, mixed = carry
                start = start_of(frame_at(i))
                at = pl.ds(pl.multiple_of(i * chunk, chunk), chunk)
                p = jnp.exp2(t_s[at, :] * slope - top)
                total = total + jnp.sum(p.reshape(chunk // 8, 8, TILE_Q), axis=0)
                p = p.astype(BF16)
                p_s[at, :] = p
                values = kv_ref[pl.ds(start, 4), 1].reshape(chunk, DH)
                mixed = mixed + lax.dot_general(
                    values, p, (((0,), (0,)), ((), ())), preferred_element_type=F32
                )
                return total, mixed

            total, mixed = lax.fori_loop(
                0, count, mix, (jnp.zeros((8, TILE_Q), F32), jnp.zeros((DH, TILE_Q), F32))
            )
            inverse = 1.0 / jnp.sum(total, axis=0, keepdims=True)
            att_t = (mixed * inverse).astype(BF16)
            att_ref[rows] = att_t.T
            do_t = (do_ref[rows].T.astype(F32) * inverse).astype(BF16)
            do_n = do_t.T
            delta = jnp.sum(do_t.astype(F32) * att_t.astype(F32), axis=0, keepdims=True)

            def back(i, dq_t):
                start = start_of(frame_at(i))
                at = pl.ds(pl.multiple_of(i * chunk, chunk), chunk)
                keys = kv_ref[pl.ds(start, 4), 0].reshape(chunk, DH)
                values = kv_ref[pl.ds(start, 4), 1].reshape(chunk, DH)
                p = p_s[at, :]
                dp = jnp.dot(values, do_t, preferred_element_type=F32)
                g = (p.astype(F32) * (dp - delta)).astype(BF16)
                dk = jnp.dot(g, q_tile, preferred_element_type=F32)
                dv = jnp.dot(p, do_n, preferred_element_type=F32)
                dk_s[pl.ds(start, 4)] += dk.reshape(4, BLK, DH)
                dv_s[pl.ds(start, 4)] += dv.reshape(4, BLK, DH)
                return dq_t + lax.dot_general(
                    keys, g, (((0,), (0,)), ((), ())), preferred_element_type=F32
                )

            dq_t = lax.fori_loop(0, count, back, jnp.zeros((DH, TILE_Q), F32))
            dq_ref[rows] = (dq_t * scale).astype(BF16).T

        @pl.loop(0, NBLK)
        def _(b):
            dkv_ref[b, 0] = (dk_s[b] * scale).astype(BF16)
            dkv_ref[b, 1] = dv_s[b].astype(BF16)


def scatter_kernel(
    att_ref, dq_ref, dkv_ref,
    atto_ref, dqo_ref, dko_ref, dvo_ref,
    got, acc, done, own_sem, out_sem, in_sem, part_send, part_sem, done_send, keep,
):
    y, place, x_lo, core = position()
    is_owner, src_head, j_there = my_task(place, x_lo, core)
    me_head = lax.axis_index("head")
    base = y * PLANE
    owners = [owner_of(j, x_lo, core) for j in range(HPD)]
    column = pl.ds(pl.multiple_of(j_there * DH, DH), DH)

    barrier = pltpu.get_barrier_semaphore()
    for there, head in owners:
        pl.semaphore_signal(barrier, inc=1, device_id=(base + there, head), device_id_type=MESH)

    @pl.when(is_owner)
    def _():
        planes = [lax.rem(y + d, RING) for d in range(RING)]
        for d in range(1, RING):
            pl.semaphore_signal(
                barrier, inc=1, device_id=(planes[d] * PLANE + place, me_head),
                device_id_type=MESH,
            )
        mine = pltpu.make_async_copy(dkv_ref.at[pl.ds(base, PLANE)], keep, own_sem)
        mine.start()
        pl.semaphore_wait(barrier, PLANE + RING - 1)

        def part_copy(d, r):
            return pltpu.make_async_remote_copy(
                src_ref=dkv_ref.at[planes[d] * PLANE + r], dst_ref=got.at[d - 1, r],
                send_sem=part_send.at[d - 1], recv_sem=part_sem.at[d - 1, r],
                device_id=(planes[d] * PLANE + place, me_head), device_id_type=MESH,
            )

        def sent_when(d):
            return y + d >= RING

        def got_when(d):
            return y < d

        for r in range(PLANE):
            for d in (2, 1, 3):
                if d == 1 and r < 3:
                    part_copy(d, r).start()
                else:
                    pl.when(sent_when(d))(lambda d=d, r=r: part_copy(d, r).start())
        for r in range(PLANE):
            for part, (ref, out) in enumerate(((att_ref, atto_ref), (dq_ref, dqo_ref))):
                pltpu.make_async_remote_copy(
                    src_ref=ref.at[pl.ds(r * BLK, BLK)], dst_ref=out.at[:, column],
                    send_sem=out_sem.at[part], recv_sem=in_sem.at[part],
                    device_id=(base + r, src_head), device_id_type=MESH,
                ).start()
        mine.wait()
        for r in range(PLANE):
            acc[...] = keep[r].astype(F32)

            def add(d, r=r):
                pltpu.make_async_copy(got.at[d - 1, r], got.at[d - 1, r], part_sem.at[d - 1, r]).wait()
                acc[...] += got[d - 1, r].astype(F32)

            for d in (1, 3, 2):
                if d == 1 and r < 3:
                    add(d)
                else:
                    pl.when(got_when(d))(lambda d=d: add(d))
            done[r] = acc[...].astype(BF16)
            for part, out in enumerate((dko_ref, dvo_ref)):
                pltpu.make_async_remote_copy(
                    src_ref=done.at[r, part], dst_ref=out.at[:, column],
                    send_sem=done_send, recv_sem=in_sem.at[2 + part],
                    device_id=(base + r, src_head), device_id_type=MESH,
                ).start()
        for part, ref in enumerate((att_ref, dq_ref)):
            pltpu.make_async_copy(ref, ref, out_sem.at[part]).wait()
        pltpu.make_async_copy(done, done, done_send).wait()

        def drained(d, count):
            some = dkv_ref.at[pl.ds(0, count)]
            pltpu.make_async_copy(some, some, part_send.at[d - 1]).wait()

        pl.when(sent_when(1))(lambda: drained(1, PLANE))
        pl.when(jnp.logical_not(sent_when(1)))(lambda: drained(1, 3))
        pl.when(sent_when(2))(lambda: drained(2, PLANE))
        pl.when(sent_when(3))(lambda: drained(3, PLANE))

    for part, ref in enumerate((atto_ref, dqo_ref, dko_ref, dvo_ref)):
        pltpu.make_async_copy(ref, ref, in_sem.at[part]).wait()


def per_device(query, key, value, grad_out, frame_ids, sink_frame, window):
    any_spec = pl.BlockSpec(memory_space=pl.ANY)
    smem = pl.BlockSpec(memory_space=pltpu.SMEM)
    vmem = pl.BlockSpec(memory_space=pltpu.VMEM)
    dma = pltpu.SemaphoreType.DMA
    shape = jax.ShapeDtypeStruct
    rows = PLANE * BLK
    windows = jnp.broadcast_to(window[:, None, None], (HPD, 8, 128))
    q_all, do_all, kv_all, w_all = pl.pallas_call(
        gather_kernel,
        out_shape=(
            shape((rows, DH), BF16),
            shape((rows, DH), BF16),
            shape((NBLK, 2, BLK, DH), BF16),
            shape((8, 128), jnp.int32),
        ),
        in_specs=[any_spec] * 5,
        out_specs=[any_spec] * 4,
        scratch_shapes=[
            dma((4,)), dma, dma((2,)), dma((PLANE,)), dma,
            dma((PLANE,)), dma((PLANE,)), dma((PLANE // 2,)), dma((PLANE // 2,)), dma((4,)),
        ],
        compiler_params=pltpu.CompilerParams(collective_id=0, has_side_effects=True),
        name="gather",
    )(query, key, value, grad_out, windows)
    att, dq, dkv = pl.pallas_call(
        attend_kernel,
        out_shape=(
            shape((rows, DH), BF16),
            shape((rows, DH), BF16),
            shape((NBLK, 2, BLK, DH), BF16),
        ),
        in_specs=[smem] * 3 + [vmem] * 3,
        out_specs=[vmem] * 3,
        scratch_shapes=[
            pltpu.VMEM((MAX_CHUNKS * 4 * BLK, TILE_Q), F32),
            pltpu.VMEM((MAX_CHUNKS * 4 * BLK, TILE_Q), BF16),
            pltpu.VMEM((NBLK, BLK, DH), F32),
            pltpu.VMEM((NBLK, BLK, DH), F32),
        ],
        name="attend",
    )(frame_ids, sink_frame, w_all, q_all, do_all, kv_all)
    return pl.pallas_call(
        scatter_kernel,
        out_shape=tuple(shape(query.shape, BF16) for _ in range(4)),
        in_specs=[any_spec] * 3,
        out_specs=[any_spec] * 4,
        scratch_shapes=[
            pltpu.VMEM((RING - 1, PLANE, 2, BLK, DH), BF16),
            pltpu.VMEM((2, BLK, DH), F32),
            pltpu.VMEM((PLANE, 2, BLK, DH), BF16),
            dma, dma((2,)), dma((4,)), dma((RING - 1,)), dma((RING - 1, PLANE)), dma,
            pltpu.VMEM((PLANE, 2, BLK, DH), BF16),
        ],
        compiler_params=pltpu.CompilerParams(collective_id=1, has_side_effects=True),
        name="scatter",
    )(att, dq, dkv)


def solution(mesh):
    tm_head = P("tm", "head")
    return jax.shard_map(
        per_device,
        mesh=mesh,
        in_specs=(tm_head, tm_head, tm_head, tm_head, P(), P(), P("head")),
        out_specs=(tm_head, tm_head, tm_head, tm_head),
        check_vma=False,
    )
```

```python
import math

import jax
import jax.numpy as jnp
from jax import lax
from jax.experimental import pallas as pl
from jax.experimental.pallas import tpu as pltpu
from jax.sharding import PartitionSpec as P

MESH = pl.DeviceIdType.MESH
BLK = 128
DH = 128
HPD = 5
RING = 4
PLANE = 8
AHEAD = 3
NBLK = RING * PLANE
BF16 = jnp.bfloat16
F32 = jnp.float32
TILE_Q = 2 * BLK
MAX_CHUNKS = 5
NEG = -1e30


def seat_of(u):
    if u < 8:
        return 2 * (u % 4) + u // 4, (u % 4 + u // 4) % 2
    return ((0, 1), (5, 0))[u - 8]


def position():
    tm = lax.axis_index("tm")
    head = lax.axis_index("head")
    return tm // PLANE, tm % PLANE, head // 2, head % 2


def owner_ids(y):
    _, _, x_lo, core = position()
    half = y // 2
    ids = []
    for j in range(HPD):
        (p0, e0), (p1, e1) = seat_of(j), seat_of(HPD + j)
        place = p0 + core * (p1 - p0)
        e = e0 + core * (e1 - e0)
        row = (1 - half) * (1 - e) + half * (2 + e)
        ids.append((row * PLANE + place, 2 * (1 - x_lo) + y % 2))
    return ids


def my_task():
    row, place, x_lo, core = position()
    half = row // 2
    e = half * (row - 2) + (1 - half) * (1 - row)
    other = (e + place // 2 + place % 2) % 2
    u = (1 - other) * (4 * (place % 2) + place // 2) + other * (8 + place // 5)
    is_owner = (other == 0) | (place == 0) | (place == 5)
    return is_owner, 2 * half + core, 2 * (1 - x_lo) + u // HPD, u % HPD


def neighbours():
    row, place, x_lo, core = position()
    tm = row * PLANE + place
    across = (RING - 1 - row) * PLANE + place
    same, swapped = 2 * x_lo + core, 2 * x_lo + 1 - core
    return (tm, swapped), (across, same), (across, swapped)


def signal(device):
    pl.semaphore_signal(
        pltpu.get_barrier_semaphore(), inc=1, device_id=device, device_id_type=MESH
    )


def wait_for(count):
    pl.semaphore_wait(pltpu.get_barrier_semaphore(), count)


def send(src, dst, send_sem, recv_sem, device):
    pltpu.make_async_remote_copy(
        src_ref=src, dst_ref=dst, send_sem=send_sem, recv_sem=recv_sem,
        device_id=device, device_id_type=MESH,
    ).start()


def settle(ref, sem):
    pltpu.make_async_copy(ref, ref, sem).wait()


def gather_kernel(
    q_ref, k_ref, v_ref, do_ref, w_ref,
    qo_ref, doo_ref, kvo_ref, wo_ref,
    send_sem, ahead_send, w_send, qd_sem, kv_sem, w_sem, ahead_sem,
    sib_sem, cross_sem, relay_sem, sib_send, cross_send, relay_send,
):
    y, place, _, _ = position()
    is_owner, plane, src_head, _ = my_task()
    sibling, across, _ = neighbours()
    even = plane % 2 == 0
    early = plane < 2
    looked_at = (y == 2) & (place < AHEAD)

    @pl.when(is_owner)
    def _():
        for r in range(PLANE):
            signal((plane * PLANE + r, src_head))
        signal(sibling)
        pl.when(jnp.logical_not(early))(lambda: signal(across))

        @pl.when(plane == 1)
        def _():
            for r in range(AHEAD):
                signal((2 * PLANE + r, src_head))

    wait_for(
        jnp.where(looked_at, 2 * HPD, HPD)
        + jnp.where(is_owner, 1, 0)
        + jnp.where(is_owner & early, 1, 0)
    )

    def column(ref, j):
        return ref.at[:, pl.ds(j * DH, DH)]

    rows = pl.ds(pl.multiple_of(place * BLK, BLK), BLK)
    targets = owner_ids(y)
    tile = y * PLANE + place
    for j in range(HPD):
        for part, ref in enumerate((k_ref, v_ref)):
            send(column(ref, j), kvo_ref.at[tile, part], send_sem.at[part], kv_sem.at[place],
                 targets[j])

    @pl.when(looked_at)
    def _():
        for j, device in enumerate(owner_ids(1)):
            for part, ref in enumerate((k_ref, v_ref)):
                send(column(ref, j), kvo_ref.at[tile, part], ahead_send.at[part],
                     ahead_sem.at[place], device)

    for j in range(HPD):
        for part, (ref, out) in enumerate(((q_ref, qo_ref), (do_ref, doo_ref))):
            send(column(ref, j), out.at[rows], send_sem.at[2 + part], qd_sem.at[part], targets[j])

    @pl.when(place == 0)
    def _():
        for j in range(HPD):
            send(w_ref, wo_ref, w_send.at[j], w_sem, targets[j])

    @pl.when(is_owner)
    def _():
        base = plane * PLANE

        def pass_on(block, to, recv, sent):
            send(kvo_ref.at[block], kvo_ref.at[block], sent, recv, to)

        for r in range(PLANE):
            settle(kvo_ref.at[base + r], kv_sem.at[r])
            pl.when(early)(lambda r=r: pass_on(base + r, across, cross_sem.at[r], cross_send))
            if r < AHEAD:
                pass_on(base + r, sibling, sib_sem.at[r], sib_send)
            else:
                pl.when(even)(lambda r=r: pass_on(base + r, sibling, sib_sem.at[r], sib_send))

        @pl.when(jnp.logical_not(early))
        def _():
            mine = (plane - 2) * PLANE
            theirs = (1 - (plane - 2)) * PLANE
            for r in range(PLANE):
                settle(kvo_ref.at[mine + r], cross_sem.at[r])
                pass_on(mine + r, sibling, relay_sem.at[r], relay_send)
            for r in range(PLANE):
                settle(kvo_ref.at[theirs + r], relay_sem.at[r])
            settle(kvo_ref.at[pl.ds(0, PLANE)], relay_send)

        beside = (plane + 1 - 2 * (plane % 2)) * PLANE
        for r in range(AHEAD):
            settle(kvo_ref.at[beside + r], sib_sem.at[r])

        @pl.when(jnp.logical_not(even))
        def _():
            for r in range(AHEAD, PLANE):
                settle(kvo_ref.at[beside + r], sib_sem.at[r])

        @pl.when(plane == 1)
        def _():
            for r in range(AHEAD):
                settle(kvo_ref.at[2 * PLANE + r], ahead_sem.at[r])

        settle(qo_ref, qd_sem.at[0])
        settle(doo_ref, qd_sem.at[1])
        settle(wo_ref, w_sem)
        pl.when(early)(lambda: settle(kvo_ref.at[pl.ds(0, PLANE)], cross_send))
        pl.when(even)(lambda: settle(kvo_ref.at[pl.ds(0, PLANE)], sib_send))
        pl.when(jnp.logical_not(even))(
            lambda: settle(kvo_ref.at[pl.ds(0, AHEAD)], sib_send)
        )

    for part, ref in enumerate((k_ref, v_ref, q_ref, do_ref)):
        settle(ref, send_sem.at[part])

    @pl.when(looked_at)
    def _():
        settle(k_ref, ahead_send.at[0])
        settle(v_ref, ahead_send.at[1])

    @pl.when(place == 0)
    def _():
        for j in range(HPD):
            settle(w_ref, w_send.at[j])


def attend_kernel(
    fid_ref, sink_ref, w_ref, q_ref, do_ref, kv_ref,
    att_ref, dq_ref, dkv_ref,
    t_s, p_s, dk_s, dv_s,
):
    is_owner, y, _, src_j = my_task()
    scale = 1.0 / math.sqrt(DH)
    slope = scale * math.log2(math.e)
    chunk = 4 * BLK

    @pl.when(is_owner)
    def _():
        c = 1 + fid_ref[1] + fid_ref[2]
        sink = sink_ref[0]
        win = w_ref[src_j]
        dk_s[...] = jnp.zeros_like(dk_s)
        dv_s[...] = jnp.zeros_like(dv_s)
        lane = lax.broadcasted_iota(jnp.int32, (1, TILE_Q), 1)

        def sees(query_frame, frame):
            near = (frame <= query_frame) & (frame > query_frame - win)
            return near | ((frame == sink) & (sink <= query_frame))

        @pl.loop(0, PLANE // 2)
        def _(t):
            rows = pl.ds(pl.multiple_of(t * TILE_Q, TILE_Q), TILE_Q)
            block_a = y * PLANE + 2 * t
            frame_a = (block_a + c) // 4
            frame_b = (block_a + 1 + c) // 4
            low = jnp.maximum(frame_a - win + 1, 0)
            near_count = frame_b - low + 1
            count = near_count + (sink < low).astype(jnp.int32)

            def frame_at(i):
                return jnp.where(i < near_count, low + i, sink)

            def start_of(frame):
                return jnp.clip(4 * frame - c, 0, NBLK - 4)

            q_tile = q_ref[rows]
            q_t = q_tile.T

            def scores(i, top):
                frame = frame_at(i)
                start = start_of(frame)
                see_a = sees(frame_a, frame)
                see_b = sees(frame_b, frame)
                keys = kv_ref[pl.ds(start, 4), 0].reshape(chunk, DH)
                s = jnp.dot(keys, q_t, preferred_element_type=F32)
                for k in range(4):
                    here = (start + k + c) // 4 == frame
                    bias = jnp.where(
                        lane < BLK,
                        jnp.where(here & see_a, 0.0, NEG),
                        jnp.where(here & see_b, 0.0, NEG),
                    )
                    part = s[k * BLK : (k + 1) * BLK] + bias
                    t_s[pl.ds(i * chunk + k * BLK, BLK), :] = part
                    top = jnp.maximum(top, jnp.max(part.reshape(BLK // 8, 8, TILE_Q), axis=0))
                return top

            top = lax.fori_loop(0, count, scores, jnp.full((8, TILE_Q), NEG, F32))
            top = jnp.max(top, axis=0, keepdims=True) * slope

            def mix(i, carry):
                total, mixed = carry
                start = start_of(frame_at(i))
                at = pl.ds(pl.multiple_of(i * chunk, chunk), chunk)
                p = jnp.exp2(t_s[at, :] * slope - top)
                total = total + jnp.sum(p.reshape(chunk // 8, 8, TILE_Q), axis=0)
                p = p.astype(BF16)
                p_s[at, :] = p
                values = kv_ref[pl.ds(start, 4), 1].reshape(chunk, DH)
                mixed = mixed + lax.dot_general(
                    values, p, (((0,), (0,)), ((), ())), preferred_element_type=F32
                )
                return total, mixed

            total, mixed = lax.fori_loop(
                0, count, mix, (jnp.zeros((8, TILE_Q), F32), jnp.zeros((DH, TILE_Q), F32))
            )
            inverse = 1.0 / jnp.sum(total, axis=0, keepdims=True)
            att_t = (mixed * inverse).astype(BF16)
            att_ref[rows] = att_t.T
            do_t = (do_ref[rows].T.astype(F32) * inverse).astype(BF16)
            do_n = do_t.T
            delta = jnp.sum(do_t.astype(F32) * att_t.astype(F32), axis=0, keepdims=True)

            def back(i, dq_t):
                start = start_of(frame_at(i))
                at = pl.ds(pl.multiple_of(i * chunk, chunk), chunk)
                keys = kv_ref[pl.ds(start, 4), 0].reshape(chunk, DH)
                values = kv_ref[pl.ds(start, 4), 1].reshape(chunk, DH)
                p = p_s[at, :]
                dp = jnp.dot(values, do_t, preferred_element_type=F32)
                g = (p.astype(F32) * (dp - delta)).astype(BF16)
                dk = jnp.dot(g, q_tile, preferred_element_type=F32)
                dv = jnp.dot(p, do_n, preferred_element_type=F32)
                dk_s[pl.ds(start, 4)] += dk.reshape(4, BLK, DH)
                dv_s[pl.ds(start, 4)] += dv.reshape(4, BLK, DH)
                return dq_t + lax.dot_general(
                    keys, g, (((0,), (0,)), ((), ())), preferred_element_type=F32
                )

            dq_t = lax.fori_loop(0, count, back, jnp.zeros((DH, TILE_Q), F32))
            dq_ref[rows] = (dq_t * scale).astype(BF16).T

        @pl.loop(0, NBLK)
        def _(b):
            dkv_ref[b, 0] = (dk_s[b] * scale).astype(BF16)
            dkv_ref[b, 1] = dv_s[b].astype(BF16)


def scatter_kernel(
    att_ref, dq_ref, dkv_ref,
    atto_ref, dqo_ref, dko_ref, dvo_ref,
    keep, beside, over, back, ahead, far, joined, done, acc,
    keep_sem, far_sem, out_send, out_sem, done_send,
    beside_send, beside_sem, over_send, over_sem, joined_send, back_sem, ahead_send, ahead_sem,
):
    y, place, _, _ = position()
    is_owner, plane, src_head, j_there = my_task()
    sibling, across, diagonal = neighbours()
    even = plane % 2 == 0
    early = plane < 2
    late = jnp.logical_not(early)
    base = plane * PLANE
    column = pl.ds(pl.multiple_of(j_there * DH, DH), DH)

    for device in owner_ids(y):
        signal(device)

    @pl.when(is_owner)
    def _():
        signal(sibling)
        pl.when(early)(lambda: signal(across))
        pl.when(plane == 2)(lambda: signal(diagonal))
        mine = pltpu.make_async_copy(dkv_ref.at[pl.ds(base, PLANE)], keep, keep_sem)
        mine.start()
        low = (plane % 2) * PLANE
        other_low = (1 - plane % 2) * PLANE
        theirs = pltpu.make_async_copy(dkv_ref.at[pl.ds(low, PLANE)], far, far_sem)
        pl.when(late)(theirs.start)
        wait_for(jnp.where(late | (plane == 1), PLANE + 2, PLANE + 1))

        next_to = (plane + 1 - 2 * (plane % 2)) * PLANE

        @pl.when(late)
        def _():
            for r in range(PLANE):
                send(dkv_ref.at[other_low + r], over.at[r], over_send, over_sem.at[r], sibling)

        for r in range(PLANE):
            def to_sibling(r=r):
                send(dkv_ref.at[next_to + r], beside.at[r], beside_send, beside_sem.at[r], sibling)

            if r < AHEAD:
                to_sibling()
            else:
                pl.when(jnp.logical_not(even))(to_sibling)

        @pl.when(plane == 1)
        def _():
            for r in range(AHEAD):
                send(dkv_ref.at[2 * PLANE + r], ahead.at[r], ahead_send, ahead_sem.at[r], diagonal)

        @pl.when(late)
        def _():
            theirs.wait()
            for r in range(PLANE):
                settle(over.at[r], over_sem.at[r])
                joined[r] = (over[r].astype(F32) + far[r].astype(F32)).astype(BF16)
                send(joined.at[r], back.at[r], joined_send, back_sem.at[r], across)

        for r in range(PLANE):
            for part, (ref, out) in enumerate(((att_ref, atto_ref), (dq_ref, dqo_ref))):
                send(ref.at[pl.ds(r * BLK, BLK)], out.at[:, column], out_send.at[part],
                     out_sem.at[part], (base + r, src_head))
        mine.wait()
        for r in range(PLANE):
            acc[...] = keep[r].astype(F32)

            def add(buffer, sems, r=r):
                settle(buffer.at[r], sems.at[r])
                acc[...] += buffer[r].astype(F32)

            if r < AHEAD:
                add(beside, beside_sem)
                pl.when(plane == 2)(lambda add=add: add(ahead, ahead_sem))
            else:
                pl.when(even)(lambda add=add: add(beside, beside_sem))
            pl.when(early)(lambda add=add: add(back, back_sem))
            done[r] = acc[...].astype(BF16)
            for part, out in enumerate((dko_ref, dvo_ref)):
                send(done.at[r, part], out.at[:, column], done_send, out_sem.at[2 + part],
                     (base + r, src_head))
        settle(att_ref, out_send.at[0])
        settle(dq_ref, out_send.at[1])
        settle(done, done_send)
        pl.when(even)(lambda: settle(ahead, beside_send))
        pl.when(jnp.logical_not(even))(lambda: settle(done, beside_send))
        pl.when(plane == 1)(lambda: settle(ahead, ahead_send))

        @pl.when(late)
        def _():
            settle(done, over_send)
            settle(joined, joined_send)

    for part, ref in enumerate((atto_ref, dqo_ref, dko_ref, dvo_ref)):
        settle(ref, out_sem.at[part])


def finish_kernel(*refs):
    for src, out in zip(refs[:4], refs[4:]):
        out[...] = src[...]


def per_device(query, key, value, grad_out, frame_ids, sink_frame, window):
    any_spec = pl.BlockSpec(memory_space=pl.ANY)
    smem = pl.BlockSpec(memory_space=pltpu.SMEM)
    vmem = pl.BlockSpec(memory_space=pltpu.VMEM)
    dma = pltpu.SemaphoreType.DMA
    shape = jax.ShapeDtypeStruct
    rows = PLANE * BLK
    q_all, do_all, kv_all, w_all = pl.pallas_call(
        gather_kernel,
        out_shape=(
            shape((rows, DH), BF16),
            shape((rows, DH), BF16),
            shape((NBLK, 2, BLK, DH), BF16),
            shape((HPD,), jnp.int32),
        ),
        in_specs=[any_spec] * 5,
        out_specs=[any_spec] * 4,
        scratch_shapes=[
            dma((4,)), dma((2,)), dma((HPD,)), dma((2,)), dma((PLANE,)), dma, dma((AHEAD,)),
            dma((PLANE,)), dma((PLANE,)), dma((PLANE,)), dma, dma, dma,
        ],
        compiler_params=pltpu.CompilerParams(collective_id=0, has_side_effects=True),
        name="gather",
    )(query, key, value, grad_out, window)
    att, dq, dkv = pl.pallas_call(
        attend_kernel,
        out_shape=(
            shape((rows, DH), BF16),
            shape((rows, DH), BF16),
            shape((NBLK, 2, BLK, DH), BF16),
        ),
        in_specs=[smem] * 3 + [vmem] * 3,
        out_specs=[vmem] * 3,
        scratch_shapes=[
            pltpu.VMEM((MAX_CHUNKS * 4 * BLK, TILE_Q), F32),
            pltpu.VMEM((MAX_CHUNKS * 4 * BLK, TILE_Q), BF16),
            pltpu.VMEM((NBLK, BLK, DH), F32),
            pltpu.VMEM((NBLK, BLK, DH), F32),
        ],
        name="attend",
    )(frame_ids, sink_frame, w_all, q_all, do_all, kv_all)

    def tiles(count):
        return pltpu.VMEM((count, 2, BLK, DH), BF16)

    outs = pl.pallas_call(
        scatter_kernel,
        out_shape=tuple(shape(query.shape, BF16) for _ in range(4)),
        in_specs=[any_spec] * 3,
        out_specs=[any_spec] * 4,
        scratch_shapes=[
            tiles(PLANE), tiles(PLANE), tiles(PLANE), tiles(PLANE), tiles(AHEAD), tiles(PLANE),
            tiles(PLANE), tiles(PLANE), pltpu.VMEM((2, BLK, DH), F32),
            dma, dma, dma((2,)), dma((4,)), dma,
            dma, dma((PLANE,)), dma, dma((PLANE,)), dma, dma((PLANE,)), dma, dma((AHEAD,)),
        ],
        compiler_params=pltpu.CompilerParams(collective_id=1, has_side_effects=True),
        name="scatter",
    )(att, dq, dkv)
    return pl.pallas_call(
        finish_kernel,
        out_shape=tuple(shape(query.shape, BF16) for _ in range(4)),
        in_specs=[vmem] * 4,
        out_specs=[vmem] * 4,
        name="finish",
    )(*outs)


def solution(mesh):
    tm_head = P("tm", "head")
    return jax.shard_map(
        per_device,
        mesh=mesh,
        in_specs=(tm_head, tm_head, tm_head, tm_head, P(), P(), P("head")),
        out_specs=(tm_head, tm_head, tm_head, tm_head),
        check_vma=False,
    )
```

```python
import math

import jax
import jax.numpy as jnp
from jax import lax
from jax.experimental import pallas as pl
from jax.experimental.pallas import tpu as pltpu
from jax.sharding import PartitionSpec as P

MESH = pl.DeviceIdType.MESH
BLK = 128
DH = 128
HPD = 5
RING = 4
PLANE = 8
AHEAD = 3
NBLK = RING * PLANE
BF16 = jnp.bfloat16
F32 = jnp.float32
TILE_Q = 2 * BLK
MAX_CHUNKS = 5
NEG = -1e30
MIB = 1 << 20


def seat_of(u):
    if u < 8:
        return 2 * (u % 4) + u // 4, (u % 4 + u // 4) % 2
    return ((0, 1), (5, 0))[u - 8]


def position():
    tm = lax.axis_index("tm")
    head = lax.axis_index("head")
    return tm // PLANE, tm % PLANE, head // 2, head % 2


def owner_ids(y):
    _, _, x_lo, core = position()
    half = y // 2
    ids = []
    for j in range(HPD):
        (p0, e0), (p1, e1) = seat_of(j), seat_of(HPD + j)
        place = p0 + core * (p1 - p0)
        e = e0 + core * (e1 - e0)
        row = (1 - half) * (1 - e) + half * (2 + e)
        ids.append((row * PLANE + place, 2 * (1 - x_lo) + y % 2))
    return ids


def my_task():
    row, place, x_lo, core = position()
    half = row // 2
    e = half * (row - 2) + (1 - half) * (1 - row)
    other = (e + place // 2 + place % 2) % 2
    u = (1 - other) * (4 * (place % 2) + place // 2) + other * (8 + place // 5)
    is_owner = (other == 0) | (place == 0) | (place == 5)
    return is_owner, 2 * half + core, 2 * (1 - x_lo) + u // HPD, u % HPD


def neighbours():
    row, place, x_lo, core = position()
    tm = row * PLANE + place
    across = (RING - 1 - row) * PLANE + place
    same, swapped = 2 * x_lo + core, 2 * x_lo + 1 - core
    return (tm, swapped), (across, same), (across, swapped)


def signal(device):
    pl.semaphore_signal(
        pltpu.get_barrier_semaphore(), inc=1, device_id=device, device_id_type=MESH
    )


def wait_for(count):
    pl.semaphore_wait(pltpu.get_barrier_semaphore(), count)


def send(src, dst, send_sem, recv_sem, device):
    pltpu.make_async_remote_copy(
        src_ref=src, dst_ref=dst, send_sem=send_sem, recv_sem=recv_sem,
        device_id=device, device_id_type=MESH,
    ).start()


def settle(ref, sem):
    pltpu.make_async_copy(ref, ref, sem).wait()


def gather_kernel(
    q_ref, k_ref, v_ref, do_ref, w_ref,
    qo_ref, doo_ref, kvo_ref, wo_ref,
    send_sem, ahead_send, w_send, qd_sem, kv_sem, w_sem, ahead_sem,
    sib_sem, cross_sem, relay_sem, sib_send, cross_send, relay_send,
):
    y, place, _, _ = position()
    is_owner, plane, src_head, _ = my_task()
    sibling, across, _ = neighbours()
    even = plane % 2 == 0
    early = plane < 2
    looked_at = (y == 2) & (place < AHEAD)

    @pl.when(is_owner)
    def _():
        for r in range(PLANE):
            signal((plane * PLANE + r, src_head))
        signal(sibling)
        pl.when(jnp.logical_not(early))(lambda: signal(across))

        @pl.when(plane == 1)
        def _():
            for r in range(AHEAD):
                signal((2 * PLANE + r, src_head))

    wait_for(
        jnp.where(looked_at, 2 * HPD, HPD)
        + jnp.where(is_owner, 1, 0)
        + jnp.where(is_owner & early, 1, 0)
    )

    def column(ref, j):
        return ref.at[:, pl.ds(j * DH, DH)]

    rows = pl.ds(pl.multiple_of(place * BLK, BLK), BLK)
    targets = owner_ids(y)
    tile = y * PLANE + place
    for j in range(HPD):
        for part, ref in enumerate((k_ref, v_ref)):
            send(column(ref, j), kvo_ref.at[tile, part], send_sem.at[part], kv_sem.at[place],
                 targets[j])

    @pl.when(looked_at)
    def _():
        for j, device in enumerate(owner_ids(1)):
            for part, ref in enumerate((k_ref, v_ref)):
                send(column(ref, j), kvo_ref.at[tile, part], ahead_send.at[part],
                     ahead_sem.at[place], device)

    for j in range(HPD):
        for part, (ref, out) in enumerate(((q_ref, qo_ref), (do_ref, doo_ref))):
            send(column(ref, j), out.at[rows], send_sem.at[2 + part], qd_sem.at[part], targets[j])

    @pl.when(place == 0)
    def _():
        for j in range(HPD):
            send(w_ref, wo_ref, w_send.at[j], w_sem, targets[j])

    @pl.when(is_owner)
    def _():
        base = plane * PLANE

        def pass_on(block, to, recv, sent):
            send(kvo_ref.at[block], kvo_ref.at[block], sent, recv, to)

        for r in range(PLANE):
            settle(kvo_ref.at[base + r], kv_sem.at[r])
            pl.when(early)(lambda r=r: pass_on(base + r, across, cross_sem.at[r], cross_send))
            if r < AHEAD:
                pass_on(base + r, sibling, sib_sem.at[r], sib_send)
            else:
                pl.when(even)(lambda r=r: pass_on(base + r, sibling, sib_sem.at[r], sib_send))

        @pl.when(jnp.logical_not(early))
        def _():
            mine = (plane - 2) * PLANE
            theirs = (1 - (plane - 2)) * PLANE
            for r in range(PLANE):
                settle(kvo_ref.at[mine + r], cross_sem.at[r])
                pass_on(mine + r, sibling, relay_sem.at[r], relay_send)
            for r in range(PLANE):
                settle(kvo_ref.at[theirs + r], relay_sem.at[r])
            settle(kvo_ref.at[pl.ds(0, PLANE)], relay_send)

        beside = (plane + 1 - 2 * (plane % 2)) * PLANE
        for r in range(AHEAD):
            settle(kvo_ref.at[beside + r], sib_sem.at[r])

        @pl.when(jnp.logical_not(even))
        def _():
            for r in range(AHEAD, PLANE):
                settle(kvo_ref.at[beside + r], sib_sem.at[r])

        @pl.when(plane == 1)
        def _():
            for r in range(AHEAD):
                settle(kvo_ref.at[2 * PLANE + r], ahead_sem.at[r])

        settle(qo_ref, qd_sem.at[0])
        settle(doo_ref, qd_sem.at[1])
        settle(wo_ref, w_sem)
        pl.when(early)(lambda: settle(kvo_ref.at[pl.ds(0, PLANE)], cross_send))
        pl.when(even)(lambda: settle(kvo_ref.at[pl.ds(0, PLANE)], sib_send))
        pl.when(jnp.logical_not(even))(
            lambda: settle(kvo_ref.at[pl.ds(0, AHEAD)], sib_send)
        )

    for part, ref in enumerate((k_ref, v_ref, q_ref, do_ref)):
        settle(ref, send_sem.at[part])

    @pl.when(looked_at)
    def _():
        settle(k_ref, ahead_send.at[0])
        settle(v_ref, ahead_send.at[1])

    @pl.when(place == 0)
    def _():
        for j in range(HPD):
            settle(w_ref, w_send.at[j])


def attend_kernel(
    fid_ref, sink_ref, w_ref, q_ref, do_ref, kv_ref,
    att_ref, dq_ref, dkv_ref,
    t_s, p_s, dk_s, dv_s,
):
    is_owner, y, _, src_j = my_task()
    scale = 1.0 / math.sqrt(DH)
    slope = scale * math.log2(math.e)
    chunk = 4 * BLK

    @pl.when(is_owner)
    def _():
        c = 1 + fid_ref[1] + fid_ref[2]
        sink = sink_ref[0]
        win = w_ref[src_j]
        dk_s[...] = jnp.zeros_like(dk_s)
        dv_s[...] = jnp.zeros_like(dv_s)
        lane = lax.broadcasted_iota(jnp.int32, (1, TILE_Q), 1)

        def sees(query_frame, frame):
            near = (frame <= query_frame) & (frame > query_frame - win)
            return near | ((frame == sink) & (sink <= query_frame))

        @pl.loop(0, PLANE // 2)
        def _(t):
            rows = pl.ds(pl.multiple_of(t * TILE_Q, TILE_Q), TILE_Q)
            block_a = y * PLANE + 2 * t
            frame_a = (block_a + c) // 4
            frame_b = (block_a + 1 + c) // 4
            low = jnp.maximum(frame_a - win + 1, 0)
            near_count = frame_b - low + 1
            count = near_count + (sink < low).astype(jnp.int32)

            def frame_at(i):
                return jnp.where(i < near_count, low + i, sink)

            def start_of(frame):
                return jnp.clip(4 * frame - c, 0, NBLK - 4)

            q_tile = q_ref[rows]
            q_t = q_tile.T

            def scores(i, top):
                frame = frame_at(i)
                start = start_of(frame)
                see_a = sees(frame_a, frame)
                see_b = sees(frame_b, frame)
                keys = kv_ref[pl.ds(start, 4), 0].reshape(chunk, DH)
                s = jnp.dot(keys, q_t, preferred_element_type=F32)
                for k in range(4):
                    here = (start + k + c) // 4 == frame
                    bias = jnp.where(
                        lane < BLK,
                        jnp.where(here & see_a, 0.0, NEG),
                        jnp.where(here & see_b, 0.0, NEG),
                    )
                    part = s[k * BLK : (k + 1) * BLK] + bias
                    t_s[pl.ds(i * chunk + k * BLK, BLK), :] = part
                    top = jnp.maximum(top, jnp.max(part.reshape(BLK // 8, 8, TILE_Q), axis=0))
                return top

            top = lax.fori_loop(0, count, scores, jnp.full((8, TILE_Q), NEG, F32))
            top = jnp.max(top, axis=0, keepdims=True) * slope

            def mix(i, carry):
                total, mixed = carry
                start = start_of(frame_at(i))
                at = pl.ds(pl.multiple_of(i * chunk, chunk), chunk)
                p = jnp.exp2(t_s[at, :] * slope - top)
                total = total + jnp.sum(p.reshape(chunk // 8, 8, TILE_Q), axis=0)
                p = p.astype(BF16)
                p_s[at, :] = p
                values = kv_ref[pl.ds(start, 4), 1].reshape(chunk, DH)
                mixed = mixed + lax.dot_general(
                    values, p, (((0,), (0,)), ((), ())), preferred_element_type=F32
                )
                return total, mixed

            total, mixed = lax.fori_loop(
                0, count, mix, (jnp.zeros((8, TILE_Q), F32), jnp.zeros((DH, TILE_Q), F32))
            )
            inverse = 1.0 / jnp.sum(total, axis=0, keepdims=True)
            att_t = (mixed * inverse).astype(BF16)
            att_ref[rows] = att_t.T
            do_t = (do_ref[rows].T.astype(F32) * inverse).astype(BF16)
            do_n = do_t.T
            delta = jnp.sum(do_t.astype(F32) * att_t.astype(F32), axis=0, keepdims=True)

            def back(i, dq_t):
                start = start_of(frame_at(i))
                at = pl.ds(pl.multiple_of(i * chunk, chunk), chunk)
                keys = kv_ref[pl.ds(start, 4), 0].reshape(chunk, DH)
                values = kv_ref[pl.ds(start, 4), 1].reshape(chunk, DH)
                p = p_s[at, :]
                dp = jnp.dot(values, do_t, preferred_element_type=F32)
                g = (p.astype(F32) * (dp - delta)).astype(BF16)
                dk = jnp.dot(g, q_tile, preferred_element_type=F32)
                dv = jnp.dot(p, do_n, preferred_element_type=F32)
                dk_s[pl.ds(start, 4)] += dk.reshape(4, BLK, DH)
                dv_s[pl.ds(start, 4)] += dv.reshape(4, BLK, DH)
                return dq_t + lax.dot_general(
                    keys, g, (((0,), (0,)), ((), ())), preferred_element_type=F32
                )

            dq_t = lax.fori_loop(0, count, back, jnp.zeros((DH, TILE_Q), F32))
            dq_ref[rows] = (dq_t * scale).astype(BF16).T

        @pl.loop(0, NBLK)
        def _(b):
            dkv_ref[b, 0] = (dk_s[b] * scale).astype(BF16)
            dkv_ref[b, 1] = dv_s[b].astype(BF16)


def scatter_kernel(
    att_ref, dq_ref, dkv_ref,
    atto_ref, dqo_ref, dko_ref, dvo_ref,
    keep, beside, over, back, ahead, far, joined, done, acc,
    keep_sem, far_sem, out_send, out_sem, done_send,
    beside_send, beside_sem, over_send, over_sem, joined_send, back_sem, ahead_send, ahead_sem,
):
    y, place, _, _ = position()
    is_owner, plane, src_head, j_there = my_task()
    sibling, across, diagonal = neighbours()
    even = plane % 2 == 0
    early = plane < 2
    late = jnp.logical_not(early)
    base = plane * PLANE
    column = pl.ds(pl.multiple_of(j_there * DH, DH), DH)

    for device in owner_ids(y):
        signal(device)

    @pl.when(is_owner)
    def _():
        signal(sibling)
        pl.when(early)(lambda: signal(across))
        pl.when(plane == 2)(lambda: signal(diagonal))
        mine = pltpu.make_async_copy(dkv_ref.at[pl.ds(base, PLANE)], keep, keep_sem)
        mine.start()
        low = (plane % 2) * PLANE
        other_low = (1 - plane % 2) * PLANE
        theirs = pltpu.make_async_copy(dkv_ref.at[pl.ds(low, PLANE)], far, far_sem)
        pl.when(late)(theirs.start)
        wait_for(jnp.where(late | (plane == 1), PLANE + 2, PLANE + 1))

        next_to = (plane + 1 - 2 * (plane % 2)) * PLANE

        @pl.when(late)
        def _():
            for r in range(PLANE):
                send(dkv_ref.at[other_low + r], over.at[r], over_send, over_sem.at[r], sibling)

        for r in range(PLANE):
            def to_sibling(r=r):
                send(dkv_ref.at[next_to + r], beside.at[r], beside_send, beside_sem.at[r], sibling)

            if r < AHEAD:
                to_sibling()
            else:
                pl.when(jnp.logical_not(even))(to_sibling)

        @pl.when(plane == 1)
        def _():
            for r in range(AHEAD):
                send(dkv_ref.at[2 * PLANE + r], ahead.at[r], ahead_send, ahead_sem.at[r], diagonal)

        for r in range(PLANE):
            for part, (ref, out) in enumerate(((att_ref, atto_ref), (dq_ref, dqo_ref))):
                send(ref.at[pl.ds(r * BLK, BLK)], out.at[:, column], out_send.at[part],
                     out_sem.at[part], (base + r, src_head))

        @pl.when(late)
        def _():
            theirs.wait()
            for r in range(PLANE):
                settle(over.at[r], over_sem.at[r])
                joined[r] = (over[r].astype(F32) + far[r].astype(F32)).astype(BF16)
                send(joined.at[r], back.at[r], joined_send, back_sem.at[r], across)

        mine.wait()
        for r in range(PLANE):
            acc[...] = keep[r].astype(F32)

            def add(buffer, sems, r=r):
                settle(buffer.at[r], sems.at[r])
                acc[...] += buffer[r].astype(F32)

            if r < AHEAD:
                add(beside, beside_sem)
                pl.when(plane == 2)(lambda add=add: add(ahead, ahead_sem))
            else:
                pl.when(even)(lambda add=add: add(beside, beside_sem))
            pl.when(early)(lambda add=add: add(back, back_sem))
            done[r] = acc[...].astype(BF16)
            for part, out in enumerate((dko_ref, dvo_ref)):
                send(done.at[r, part], out.at[:, column], done_send, out_sem.at[2 + part],
                     (base + r, src_head))
        settle(att_ref, out_send.at[0])
        settle(dq_ref, out_send.at[1])
        settle(done, done_send)
        pl.when(even)(lambda: settle(ahead, beside_send))
        pl.when(jnp.logical_not(even))(lambda: settle(done, beside_send))
        pl.when(plane == 1)(lambda: settle(ahead, ahead_send))

        @pl.when(late)
        def _():
            settle(done, over_send)
            settle(joined, joined_send)

    for part, ref in enumerate((atto_ref, dqo_ref, dko_ref, dvo_ref)):
        settle(ref, out_sem.at[part])


def finish_kernel(*refs):
    for src, out in zip(refs[:4], refs[4:]):
        out[...] = src[...]


def in_vmem(array):
    return pltpu.with_memory_space_constraint(array, pltpu.VMEM)


def in_hbm(array):
    return pltpu.with_memory_space_constraint(array, pltpu.HBM)


def per_device(query, key, value, grad_out, frame_ids, sink_frame, window):
    any_spec = pl.BlockSpec(memory_space=pl.ANY)
    smem = pl.BlockSpec(memory_space=pltpu.SMEM)
    vmem = pl.BlockSpec(memory_space=pltpu.VMEM)
    dma = pltpu.SemaphoreType.DMA
    shape = jax.ShapeDtypeStruct
    rows = PLANE * BLK
    q_all, do_all, kv_all, w_all = pl.pallas_call(
        gather_kernel,
        out_shape=(
            pltpu.VMEM((rows, DH), BF16),
            pltpu.VMEM((rows, DH), BF16),
            pltpu.VMEM((NBLK, 2, BLK, DH), BF16),
            shape((HPD,), jnp.int32),
        ),
        in_specs=[any_spec] * 5,
        out_specs=[any_spec] * 4,
        scratch_shapes=[
            dma((4,)), dma((2,)), dma((HPD,)), dma((2,)), dma((PLANE,)), dma, dma((AHEAD,)),
            dma((PLANE,)), dma((PLANE,)), dma((PLANE,)), dma, dma, dma,
        ],
        compiler_params=pltpu.CompilerParams(
            collective_id=0, has_side_effects=True, vmem_limit_bytes=8 * MIB
        ),
        name="gather",
    )(*[in_hbm(array) for array in (query, key, value, grad_out, window)])
    att, dq, dkv = pl.pallas_call(
        attend_kernel,
        out_shape=(
            pltpu.VMEM((rows, DH), BF16),
            pltpu.VMEM((rows, DH), BF16),
            pltpu.VMEM((NBLK, 2, BLK, DH), BF16),
        ),
        in_specs=[smem] * 3 + [vmem] * 3,
        out_specs=[vmem] * 3,
        scratch_shapes=[
            pltpu.VMEM((MAX_CHUNKS * 4 * BLK, TILE_Q), F32),
            pltpu.VMEM((MAX_CHUNKS * 4 * BLK, TILE_Q), BF16),
            pltpu.VMEM((NBLK, BLK, DH), F32),
            pltpu.VMEM((NBLK, BLK, DH), F32),
        ],
        compiler_params=pltpu.CompilerParams(vmem_limit_bytes=32 * MIB),
        name="attend",
    )(in_hbm(frame_ids), sink_frame, w_all, in_vmem(q_all), in_vmem(do_all), in_vmem(kv_all))

    def tiles(count):
        return pltpu.VMEM((count, 2, BLK, DH), BF16)

    outs = pl.pallas_call(
        scatter_kernel,
        out_shape=tuple(pltpu.VMEM(query.shape, BF16) for _ in range(4)),
        in_specs=[any_spec] * 3,
        out_specs=[any_spec] * 4,
        scratch_shapes=[
            tiles(PLANE), tiles(PLANE), tiles(PLANE), tiles(PLANE), tiles(AHEAD), tiles(PLANE),
            tiles(PLANE), tiles(PLANE), pltpu.VMEM((2, BLK, DH), F32),
            dma, dma, dma((2,)), dma((4,)), dma,
            dma, dma((PLANE,)), dma, dma((PLANE,)), dma, dma((PLANE,)), dma, dma((AHEAD,)),
        ],
        compiler_params=pltpu.CompilerParams(
            collective_id=1, has_side_effects=True, vmem_limit_bytes=16 * MIB
        ),
        name="scatter",
    )(in_vmem(att), in_vmem(dq), in_vmem(dkv))
    return pl.pallas_call(
        finish_kernel,
        out_shape=tuple(shape(query.shape, BF16) for _ in range(4)),
        in_specs=[vmem] * 4,
        out_specs=[vmem] * 4,
        compiler_params=pltpu.CompilerParams(vmem_limit_bytes=8 * MIB),
        name="finish",
    )(*[in_vmem(out) for out in outs])


def solution(mesh):
    tm_head = P("tm", "head")
    return jax.shard_map(
        per_device,
        mesh=mesh,
        in_specs=(tm_head, tm_head, tm_head, tm_head, P(), P(), P("head")),
        out_specs=(tm_head, tm_head, tm_head, tm_head),
        check_vma=False,
    )
```

```python
import math

import jax
import jax.numpy as jnp
from jax import lax
from jax.experimental import pallas as pl
from jax.experimental.pallas import tpu as pltpu
from jax.sharding import PartitionSpec as P

MESH = pl.DeviceIdType.MESH
BLK = 128
DH = 128
HPD = 5
RING = 4
PLANE = 8
AHEAD = 3
NBLK = RING * PLANE
BF16 = jnp.bfloat16
F32 = jnp.float32
TILE_Q = 2 * BLK
MAX_CHUNKS = 5
NEG = -1e30
MIB = 1 << 20


def seat_of(u):
    if u < 8:
        return 2 * (u % 4) + u // 4, (u % 4 + u // 4) % 2
    return ((0, 1), (5, 0))[u - 8]


def position():
    tm = lax.axis_index("tm")
    head = lax.axis_index("head")
    return tm // PLANE, tm % PLANE, head // 2, head % 2


def owner_ids(y):
    _, _, x_lo, core = position()
    half = y // 2
    ids = []
    for j in range(HPD):
        (p0, e0), (p1, e1) = seat_of(j), seat_of(HPD + j)
        place = p0 + core * (p1 - p0)
        e = e0 + core * (e1 - e0)
        row = (1 - half) * (1 - e) + half * (2 + e)
        ids.append((row * PLANE + place, 2 * (1 - x_lo) + y % 2))
    return ids


def my_task():
    row, place, x_lo, core = position()
    half = row // 2
    e = half * (row - 2) + (1 - half) * (1 - row)
    other = (e + place // 2 + place % 2) % 2
    u = (1 - other) * (4 * (place % 2) + place // 2) + other * (8 + place // 5)
    is_owner = (other == 0) | (place == 0) | (place == 5)
    return is_owner, 2 * half + core, 2 * (1 - x_lo) + u // HPD, u % HPD


def neighbours():
    row, place, x_lo, core = position()
    tm = row * PLANE + place
    across = (RING - 1 - row) * PLANE + place
    same, swapped = 2 * x_lo + core, 2 * x_lo + 1 - core
    return (tm, swapped), (across, same), (across, swapped)


def signal(device):
    pl.semaphore_signal(
        pltpu.get_barrier_semaphore(), inc=1, device_id=device, device_id_type=MESH
    )


def wait_for(count):
    pl.semaphore_wait(pltpu.get_barrier_semaphore(), count)


def send(src, dst, send_sem, recv_sem, device):
    pltpu.make_async_remote_copy(
        src_ref=src, dst_ref=dst, send_sem=send_sem, recv_sem=recv_sem,
        device_id=device, device_id_type=MESH,
    ).start()


def settle(ref, sem):
    pltpu.make_async_copy(ref, ref, sem).wait()


def gather_kernel(
    q_ref, k_ref, v_ref, do_ref, w_ref,
    qo_ref, doo_ref, kvo_ref, wo_ref,
    send_sem, ahead_send, w_send, qd_sem, kv_sem, w_sem, ahead_sem,
    sib_sem, cross_sem, relay_sem, sib_send, cross_send, relay_send,
):
    y, place, _, _ = position()
    is_owner, plane, src_head, _ = my_task()
    sibling, across, _ = neighbours()
    even = plane % 2 == 0
    early = plane < 2
    looked_at = (y == 2) & (place < AHEAD)

    @pl.when(is_owner)
    def _():
        for r in range(PLANE):
            signal((plane * PLANE + r, src_head))
        signal(sibling)
        pl.when(jnp.logical_not(early))(lambda: signal(across))

        @pl.when(plane == 1)
        def _():
            for r in range(AHEAD):
                signal((2 * PLANE + r, src_head))

    wait_for(
        jnp.where(looked_at, 2 * HPD, HPD)
        + jnp.where(is_owner, 1, 0)
        + jnp.where(is_owner & early, 1, 0)
    )

    def column(ref, j):
        return ref.at[:, pl.ds(j * DH, DH)]

    rows = pl.ds(pl.multiple_of(place * BLK, BLK), BLK)
    targets = owner_ids(y)
    tile = y * PLANE + place
    for j in range(HPD):
        for part, ref in enumerate((k_ref, v_ref)):
            send(column(ref, j), kvo_ref.at[tile, part], send_sem.at[part], kv_sem.at[place],
                 targets[j])

    @pl.when(looked_at)
    def _():
        for j, device in enumerate(owner_ids(1)):
            for part, ref in enumerate((k_ref, v_ref)):
                send(column(ref, j), kvo_ref.at[tile, part], ahead_send.at[part],
                     ahead_sem.at[place], device)

    for j in range(HPD):
        for part, (ref, out) in enumerate(((q_ref, qo_ref), (do_ref, doo_ref))):
            send(column(ref, j), out.at[rows], send_sem.at[2 + part], qd_sem.at[part], targets[j])

    @pl.when(place == 0)
    def _():
        for j in range(HPD):
            send(w_ref, wo_ref, w_send.at[j], w_sem, targets[j])

    @pl.when(is_owner)
    def _():
        base = plane * PLANE

        def pass_on(block, to, recv, sent):
            send(kvo_ref.at[block], kvo_ref.at[block], sent, recv, to)

        for r in range(PLANE):
            settle(kvo_ref.at[base + r], kv_sem.at[r])
            pl.when(early)(lambda r=r: pass_on(base + r, across, cross_sem.at[r], cross_send))
            if r < AHEAD:
                pass_on(base + r, sibling, sib_sem.at[r], sib_send)
            else:
                pl.when(even)(lambda r=r: pass_on(base + r, sibling, sib_sem.at[r], sib_send))

        @pl.when(jnp.logical_not(early))
        def _():
            mine = (plane - 2) * PLANE
            theirs = (1 - (plane - 2)) * PLANE
            for r in range(PLANE):
                settle(kvo_ref.at[mine + r], cross_sem.at[r])
                pass_on(mine + r, sibling, relay_sem.at[r], relay_send)
            for r in range(PLANE):
                settle(kvo_ref.at[theirs + r], relay_sem.at[r])
            settle(kvo_ref.at[pl.ds(0, PLANE)], relay_send)

        beside = (plane + 1 - 2 * (plane % 2)) * PLANE
        for r in range(AHEAD):
            settle(kvo_ref.at[beside + r], sib_sem.at[r])

        @pl.when(jnp.logical_not(even))
        def _():
            for r in range(AHEAD, PLANE):
                settle(kvo_ref.at[beside + r], sib_sem.at[r])

        @pl.when(plane == 1)
        def _():
            for r in range(AHEAD):
                settle(kvo_ref.at[2 * PLANE + r], ahead_sem.at[r])

        settle(qo_ref, qd_sem.at[0])
        settle(doo_ref, qd_sem.at[1])
        settle(wo_ref, w_sem)
        pl.when(early)(lambda: settle(kvo_ref.at[pl.ds(0, PLANE)], cross_send))
        pl.when(even)(lambda: settle(kvo_ref.at[pl.ds(0, PLANE)], sib_send))
        pl.when(jnp.logical_not(even))(
            lambda: settle(kvo_ref.at[pl.ds(0, AHEAD)], sib_send)
        )

    for part, ref in enumerate((k_ref, v_ref, q_ref, do_ref)):
        settle(ref, send_sem.at[part])

    @pl.when(looked_at)
    def _():
        settle(k_ref, ahead_send.at[0])
        settle(v_ref, ahead_send.at[1])

    @pl.when(place == 0)
    def _():
        for j in range(HPD):
            settle(w_ref, w_send.at[j])


def attend_kernel(
    fid_ref, sink_ref, w_ref, q_ref, do_ref, kv_ref,
    att_ref, dq_ref, dkv_ref,
    t_s, p_s, dk_s, dv_s,
):
    is_owner, y, _, src_j = my_task()
    scale = 1.0 / math.sqrt(DH)
    slope = scale * math.log2(math.e)
    chunk = 4 * BLK

    @pl.when(is_owner)
    def _():
        c = 1 + fid_ref[1] + fid_ref[2]
        sink = sink_ref[0]
        win = w_ref[src_j]
        dk_s[...] = jnp.zeros_like(dk_s)
        dv_s[...] = jnp.zeros_like(dv_s)
        lane = lax.broadcasted_iota(jnp.int32, (1, TILE_Q), 1)

        def sees(query_frame, frame):
            near = (frame <= query_frame) & (frame > query_frame - win)
            return near | ((frame == sink) & (sink <= query_frame))

        @pl.loop(0, PLANE // 2)
        def _(t):
            rows = pl.ds(pl.multiple_of(t * TILE_Q, TILE_Q), TILE_Q)
            block_a = y * PLANE + 2 * t
            frame_a = (block_a + c) // 4
            frame_b = (block_a + 1 + c) // 4
            low = jnp.maximum(frame_a - win + 1, 0)
            near_count = frame_b - low + 1
            count = near_count + (sink < low).astype(jnp.int32)

            def frame_at(i):
                return jnp.where(i < near_count, low + i, sink)

            def start_of(frame):
                return jnp.clip(4 * frame - c, 0, NBLK - 4)

            q_tile = q_ref[rows]
            q_t = q_tile.T

            def scores(i, top):
                frame = frame_at(i)
                start = start_of(frame)
                see_a = sees(frame_a, frame)
                see_b = sees(frame_b, frame)
                keys = kv_ref[pl.ds(start, 4), 0].reshape(chunk, DH)
                s = jnp.dot(keys, q_t, preferred_element_type=F32)
                for k in range(4):
                    here = (start + k + c) // 4 == frame
                    bias = jnp.where(
                        lane < BLK,
                        jnp.where(here & see_a, 0.0, NEG),
                        jnp.where(here & see_b, 0.0, NEG),
                    )
                    part = s[k * BLK : (k + 1) * BLK] + bias
                    t_s[pl.ds(i * chunk + k * BLK, BLK), :] = part
                    top = jnp.maximum(top, jnp.max(part.reshape(BLK // 8, 8, TILE_Q), axis=0))
                return top

            top = lax.fori_loop(0, count, scores, jnp.full((8, TILE_Q), NEG, F32))
            top = jnp.max(top, axis=0, keepdims=True) * slope

            def mix(i, carry):
                total, mixed = carry
                start = start_of(frame_at(i))
                at = pl.ds(pl.multiple_of(i * chunk, chunk), chunk)
                p = jnp.exp2(t_s[at, :] * slope - top)
                total = total + jnp.sum(p.reshape(chunk // 8, 8, TILE_Q), axis=0)
                p = p.astype(BF16)
                p_s[at, :] = p
                values = kv_ref[pl.ds(start, 4), 1].reshape(chunk, DH)
                mixed = mixed + lax.dot_general(
                    values, p, (((0,), (0,)), ((), ())), preferred_element_type=F32
                )
                return total, mixed

            total, mixed = lax.fori_loop(
                0, count, mix, (jnp.zeros((8, TILE_Q), F32), jnp.zeros((DH, TILE_Q), F32))
            )
            inverse = 1.0 / jnp.sum(total, axis=0, keepdims=True)
            att_t = (mixed * inverse).astype(BF16)
            att_ref[rows] = att_t.T
            do_t = (do_ref[rows].T.astype(F32) * inverse).astype(BF16)
            do_n = do_t.T
            delta = jnp.sum(do_t.astype(F32) * att_t.astype(F32), axis=0, keepdims=True)

            def back(i, dq_t):
                start = start_of(frame_at(i))
                at = pl.ds(pl.multiple_of(i * chunk, chunk), chunk)
                keys = kv_ref[pl.ds(start, 4), 0].reshape(chunk, DH)
                values = kv_ref[pl.ds(start, 4), 1].reshape(chunk, DH)
                p = p_s[at, :]
                dp = jnp.dot(values, do_t, preferred_element_type=F32)
                g = (p.astype(F32) * (dp - delta)).astype(BF16)
                dk = jnp.dot(g, q_tile, preferred_element_type=F32)
                dv = jnp.dot(p, do_n, preferred_element_type=F32)
                dk_s[pl.ds(start, 4)] += dk.reshape(4, BLK, DH)
                dv_s[pl.ds(start, 4)] += dv.reshape(4, BLK, DH)
                return dq_t + lax.dot_general(
                    keys, g, (((0,), (0,)), ((), ())), preferred_element_type=F32
                )

            dq_t = lax.fori_loop(0, count, back, jnp.zeros((DH, TILE_Q), F32))
            dq_ref[rows] = (dq_t * scale).astype(BF16).T

        @pl.loop(0, NBLK)
        def _(b):
            dkv_ref[b, 0] = (dk_s[b] * scale).astype(BF16)
            dkv_ref[b, 1] = dv_s[b].astype(BF16)


def scatter_kernel(
    att_ref, dq_ref, dkv_ref,
    atto_ref, dqo_ref, dko_ref, dvo_ref,
    beside, over, back, ahead, joined, done, acc,
    out_send, out_sem, done_send,
    beside_send, beside_sem, over_send, over_sem, joined_send, back_sem, ahead_send, ahead_sem,
):
    y, place, _, _ = position()
    is_owner, plane, src_head, j_there = my_task()
    sibling, across, diagonal = neighbours()
    even = plane % 2 == 0
    early = plane < 2
    late = jnp.logical_not(early)
    base = plane * PLANE
    column = pl.ds(pl.multiple_of(j_there * DH, DH), DH)

    for device in owner_ids(y):
        signal(device)

    @pl.when(is_owner)
    def _():
        signal(sibling)
        pl.when(early)(lambda: signal(across))
        pl.when(plane == 2)(lambda: signal(diagonal))
        low = (plane % 2) * PLANE
        other_low = (1 - plane % 2) * PLANE
        wait_for(jnp.where(late | (plane == 1), PLANE + 2, PLANE + 1))

        next_to = (plane + 1 - 2 * (plane % 2)) * PLANE

        @pl.when(late)
        def _():
            for r in range(PLANE):
                send(dkv_ref.at[other_low + r], over.at[r], over_send, over_sem.at[r], sibling)

        @pl.when(late)
        def _():
            for r in range(PLANE):
                settle(over.at[r], over_sem.at[r])
                joined[r] = (over[r].astype(F32) + dkv_ref[low + r].astype(F32)).astype(BF16)
                send(joined.at[r], back.at[r], joined_send, back_sem.at[r], across)

        for r in range(PLANE):
            def to_sibling(r=r):
                send(dkv_ref.at[next_to + r], beside.at[r], beside_send, beside_sem.at[r], sibling)

            if r < AHEAD:
                to_sibling()
            else:
                pl.when(jnp.logical_not(even))(to_sibling)

        @pl.when(plane == 1)
        def _():
            for r in range(AHEAD):
                send(dkv_ref.at[2 * PLANE + r], ahead.at[r], ahead_send, ahead_sem.at[r], diagonal)

        for r in range(PLANE):
            for part, (ref, out) in enumerate(((att_ref, atto_ref), (dq_ref, dqo_ref))):
                send(ref.at[pl.ds(r * BLK, BLK)], out.at[:, column], out_send.at[part],
                     out_sem.at[part], (base + r, src_head))

        for r in range(PLANE):
            acc[...] = dkv_ref[base + r].astype(F32)

            def add(buffer, sems, r=r):
                settle(buffer.at[r], sems.at[r])
                acc[...] += buffer[r].astype(F32)

            if r < AHEAD:
                add(beside, beside_sem)
                pl.when(plane == 2)(lambda add=add: add(ahead, ahead_sem))
            else:
                pl.when(even)(lambda add=add: add(beside, beside_sem))
            pl.when(early)(lambda add=add: add(back, back_sem))
            done[r] = acc[...].astype(BF16)
            for part, out in enumerate((dko_ref, dvo_ref)):
                send(done.at[r, part], out.at[:, column], done_send, out_sem.at[2 + part],
                     (base + r, src_head))
        settle(att_ref, out_send.at[0])
        settle(dq_ref, out_send.at[1])
        settle(done, done_send)
        pl.when(even)(lambda: settle(ahead, beside_send))
        pl.when(jnp.logical_not(even))(lambda: settle(done, beside_send))
        pl.when(plane == 1)(lambda: settle(ahead, ahead_send))

        @pl.when(late)
        def _():
            settle(done, over_send)
            settle(joined, joined_send)

    for part, ref in enumerate((atto_ref, dqo_ref, dko_ref, dvo_ref)):
        settle(ref, out_sem.at[part])


def finish_kernel(*refs):
    for src, out in zip(refs[:4], refs[4:]):
        out[...] = src[...]


def in_vmem(array):
    return pltpu.with_memory_space_constraint(array, pltpu.VMEM)


def in_hbm(array):
    return pltpu.with_memory_space_constraint(array, pltpu.HBM)


def per_device(query, key, value, grad_out, frame_ids, sink_frame, window):
    any_spec = pl.BlockSpec(memory_space=pl.ANY)
    smem = pl.BlockSpec(memory_space=pltpu.SMEM)
    vmem = pl.BlockSpec(memory_space=pltpu.VMEM)
    dma = pltpu.SemaphoreType.DMA
    shape = jax.ShapeDtypeStruct
    rows = PLANE * BLK
    q_all, do_all, kv_all, w_all = pl.pallas_call(
        gather_kernel,
        out_shape=(
            pltpu.VMEM((rows, DH), BF16),
            pltpu.VMEM((rows, DH), BF16),
            pltpu.VMEM((NBLK, 2, BLK, DH), BF16),
            shape((HPD,), jnp.int32),
        ),
        in_specs=[any_spec] * 5,
        out_specs=[any_spec] * 4,
        scratch_shapes=[
            dma((4,)), dma((2,)), dma((HPD,)), dma((2,)), dma((PLANE,)), dma, dma((AHEAD,)),
            dma((PLANE,)), dma((PLANE,)), dma((PLANE,)), dma, dma, dma,
        ],
        compiler_params=pltpu.CompilerParams(
            collective_id=0, has_side_effects=True, vmem_limit_bytes=8 * MIB
        ),
        name="gather",
    )(*[in_hbm(array) for array in (query, key, value, grad_out, window)])
    att, dq, dkv = pl.pallas_call(
        attend_kernel,
        out_shape=(
            pltpu.VMEM((rows, DH), BF16),
            pltpu.VMEM((rows, DH), BF16),
            pltpu.VMEM((NBLK, 2, BLK, DH), BF16),
        ),
        in_specs=[smem] * 3 + [vmem] * 3,
        out_specs=[vmem] * 3,
        scratch_shapes=[
            pltpu.VMEM((MAX_CHUNKS * 4 * BLK, TILE_Q), F32),
            pltpu.VMEM((MAX_CHUNKS * 4 * BLK, TILE_Q), BF16),
            pltpu.VMEM((NBLK, BLK, DH), F32),
            pltpu.VMEM((NBLK, BLK, DH), F32),
        ],
        compiler_params=pltpu.CompilerParams(vmem_limit_bytes=32 * MIB),
        name="attend",
    )(in_hbm(frame_ids), sink_frame, w_all, in_vmem(q_all), in_vmem(do_all), in_vmem(kv_all))

    def tiles(count):
        return pltpu.VMEM((count, 2, BLK, DH), BF16)

    outs = pl.pallas_call(
        scatter_kernel,
        out_shape=tuple(pltpu.VMEM(query.shape, BF16) for _ in range(4)),
        in_specs=[any_spec, any_spec, vmem],
        out_specs=[any_spec] * 4,
        scratch_shapes=[
            tiles(PLANE), tiles(PLANE), tiles(PLANE), tiles(AHEAD), tiles(PLANE), tiles(PLANE),
            pltpu.VMEM((2, BLK, DH), F32),
            dma((2,)), dma((4,)), dma,
            dma, dma((PLANE,)), dma, dma((PLANE,)), dma, dma((PLANE,)), dma, dma((AHEAD,)),
        ],
        compiler_params=pltpu.CompilerParams(
            collective_id=1, has_side_effects=True, vmem_limit_bytes=16 * MIB
        ),
        name="scatter",
    )(in_vmem(att), in_vmem(dq), in_vmem(dkv))
    return pl.pallas_call(
        finish_kernel,
        out_shape=tuple(shape(query.shape, BF16) for _ in range(4)),
        in_specs=[vmem] * 4,
        out_specs=[vmem] * 4,
        compiler_params=pltpu.CompilerParams(vmem_limit_bytes=8 * MIB),
        name="finish",
    )(*[in_vmem(out) for out in outs])


def solution(mesh):
    tm_head = P("tm", "head")
    return jax.shard_map(
        per_device,
        mesh=mesh,
        in_specs=(tm_head, tm_head, tm_head, tm_head, P(), P(), P("head")),
        out_specs=(tm_head, tm_head, tm_head, tm_head),
        check_vma=False,
    )
```

```python
import math

import jax
import jax.numpy as jnp
from jax import lax
from jax.experimental import pallas as pl
from jax.experimental.pallas import tpu as pltpu
from jax.sharding import PartitionSpec as P

MESH = pl.DeviceIdType.MESH
BLK = 128
DH = 128
HPD = 5
RING = 4
PLANE = 8
AHEAD = 3
NBLK = RING * PLANE
BF16 = jnp.bfloat16
F32 = jnp.float32
TILE_Q = 4 * BLK
MAX_CHUNKS = 5
NEG = -1e30
MIB = 1 << 20


def seat_of(u):
    if u < 8:
        return 2 * (u % 4) + u // 4, (u % 4 + u // 4) % 2
    return ((0, 1), (5, 0))[u - 8]


def position():
    tm = lax.axis_index("tm")
    head = lax.axis_index("head")
    return tm // PLANE, tm % PLANE, head // 2, head % 2


def owner_ids(y):
    _, _, x_lo, core = position()
    half = y // 2
    ids = []
    for j in range(HPD):
        (p0, e0), (p1, e1) = seat_of(j), seat_of(HPD + j)
        place = p0 + core * (p1 - p0)
        e = e0 + core * (e1 - e0)
        row = (1 - half) * (1 - e) + half * (2 + e)
        ids.append((row * PLANE + place, 2 * (1 - x_lo) + y % 2))
    return ids


def my_task():
    row, place, x_lo, core = position()
    half = row // 2
    e = half * (row - 2) + (1 - half) * (1 - row)
    other = (e + place // 2 + place % 2) % 2
    u = (1 - other) * (4 * (place % 2) + place // 2) + other * (8 + place // 5)
    is_owner = (other == 0) | (place == 0) | (place == 5)
    return is_owner, 2 * half + core, 2 * (1 - x_lo) + u // HPD, u % HPD


def neighbours():
    row, place, x_lo, core = position()
    tm = row * PLANE + place
    across = (RING - 1 - row) * PLANE + place
    same, swapped = 2 * x_lo + core, 2 * x_lo + 1 - core
    return (tm, swapped), (across, same), (across, swapped)


def signal(device):
    pl.semaphore_signal(
        pltpu.get_barrier_semaphore(), inc=1, device_id=device, device_id_type=MESH
    )


def wait_for(count):
    pl.semaphore_wait(pltpu.get_barrier_semaphore(), count)


def send(src, dst, send_sem, recv_sem, device):
    pltpu.make_async_remote_copy(
        src_ref=src, dst_ref=dst, send_sem=send_sem, recv_sem=recv_sem,
        device_id=device, device_id_type=MESH,
    ).start()


def settle(ref, sem):
    pltpu.make_async_copy(ref, ref, sem).wait()


def gather_kernel(
    q_ref, k_ref, v_ref, do_ref, w_ref,
    qo_ref, doo_ref, kvo_ref, wo_ref,
    send_sem, ahead_send, w_send, qd_sem, kv_sem, w_sem, ahead_sem,
    sib_sem, cross_sem, relay_sem, sib_send, cross_send, relay_send,
):
    y, place, _, _ = position()
    is_owner, plane, src_head, _ = my_task()
    sibling, across, _ = neighbours()
    even = plane % 2 == 0
    early = plane < 2
    looked_at = (y == 2) & (place < AHEAD)

    @pl.when(is_owner)
    def _():
        for r in range(PLANE):
            signal((plane * PLANE + r, src_head))
        signal(sibling)
        pl.when(jnp.logical_not(early))(lambda: signal(across))

        @pl.when(plane == 1)
        def _():
            for r in range(AHEAD):
                signal((2 * PLANE + r, src_head))

    wait_for(
        jnp.where(looked_at, 2 * HPD, HPD)
        + jnp.where(is_owner, 1, 0)
        + jnp.where(is_owner & early, 1, 0)
    )

    def column(ref, j):
        return ref.at[:, pl.ds(j * DH, DH)]

    rows = pl.ds(pl.multiple_of(place * BLK, BLK), BLK)
    targets = owner_ids(y)
    tile = y * PLANE + place
    for j in range(HPD):
        for part, ref in enumerate((k_ref, v_ref)):
            send(column(ref, j), kvo_ref.at[tile, part], send_sem.at[part], kv_sem.at[place],
                 targets[j])

    @pl.when(looked_at)
    def _():
        for j, device in enumerate(owner_ids(1)):
            for part, ref in enumerate((k_ref, v_ref)):
                send(column(ref, j), kvo_ref.at[tile, part], ahead_send.at[part],
                     ahead_sem.at[place], device)

    for j in range(HPD):
        for part, (ref, out) in enumerate(((q_ref, qo_ref), (do_ref, doo_ref))):
            send(column(ref, j), out.at[rows], send_sem.at[2 + part], qd_sem.at[part], targets[j])

    @pl.when(place == 0)
    def _():
        for j in range(HPD):
            send(w_ref, wo_ref, w_send.at[j], w_sem, targets[j])

    @pl.when(is_owner)
    def _():
        base = plane * PLANE

        def pass_on(block, to, recv, sent):
            send(kvo_ref.at[block], kvo_ref.at[block], sent, recv, to)

        for r in range(PLANE):
            settle(kvo_ref.at[base + r], kv_sem.at[r])
            pl.when(early)(lambda r=r: pass_on(base + r, across, cross_sem.at[r], cross_send))
            if r < AHEAD:
                pass_on(base + r, sibling, sib_sem.at[r], sib_send)
            else:
                pl.when(even)(lambda r=r: pass_on(base + r, sibling, sib_sem.at[r], sib_send))

        @pl.when(jnp.logical_not(early))
        def _():
            mine = (plane - 2) * PLANE
            theirs = (1 - (plane - 2)) * PLANE
            for r in range(PLANE):
                settle(kvo_ref.at[mine + r], cross_sem.at[r])
                pass_on(mine + r, sibling, relay_sem.at[r], relay_send)
            for r in range(PLANE):
                settle(kvo_ref.at[theirs + r], relay_sem.at[r])
            settle(kvo_ref.at[pl.ds(0, PLANE)], relay_send)

        beside = (plane + 1 - 2 * (plane % 2)) * PLANE
        for r in range(AHEAD):
            settle(kvo_ref.at[beside + r], sib_sem.at[r])

        @pl.when(jnp.logical_not(even))
        def _():
            for r in range(AHEAD, PLANE):
                settle(kvo_ref.at[beside + r], sib_sem.at[r])

        @pl.when(plane == 1)
        def _():
            for r in range(AHEAD):
                settle(kvo_ref.at[2 * PLANE + r], ahead_sem.at[r])

        settle(qo_ref, qd_sem.at[0])
        settle(doo_ref, qd_sem.at[1])
        settle(wo_ref, w_sem)
        pl.when(early)(lambda: settle(kvo_ref.at[pl.ds(0, PLANE)], cross_send))
        pl.when(even)(lambda: settle(kvo_ref.at[pl.ds(0, PLANE)], sib_send))
        pl.when(jnp.logical_not(even))(
            lambda: settle(kvo_ref.at[pl.ds(0, AHEAD)], sib_send)
        )

    for part, ref in enumerate((k_ref, v_ref, q_ref, do_ref)):
        settle(ref, send_sem.at[part])

    @pl.when(looked_at)
    def _():
        settle(k_ref, ahead_send.at[0])
        settle(v_ref, ahead_send.at[1])

    @pl.when(place == 0)
    def _():
        for j in range(HPD):
            settle(w_ref, w_send.at[j])


def attend_kernel(
    fid_ref, sink_ref, w_ref, q_ref, do_ref, kv_ref,
    att_ref, dq_ref, dkv_ref,
    t_s, p_s, dk_s, dv_s,
):
    is_owner, y, _, src_j = my_task()
    scale = 1.0 / math.sqrt(DH)
    slope = scale * math.log2(math.e)
    chunk = 4 * BLK

    @pl.when(is_owner)
    def _():
        c = 1 + fid_ref[1] + fid_ref[2]
        sink = sink_ref[0]
        win = w_ref[src_j]
        dk_s[...] = jnp.zeros_like(dk_s)
        dv_s[...] = jnp.zeros_like(dv_s)
        lane = lax.broadcasted_iota(jnp.int32, (1, TILE_Q), 1)

        def sees(query_frame, frame):
            near = (frame <= query_frame) & (frame > query_frame - win)
            return near | ((frame == sink) & (sink <= query_frame))

        @pl.loop(0, PLANE // 4)
        def _(t):
            rows = pl.ds(pl.multiple_of(t * TILE_Q, TILE_Q), TILE_Q)
            frame_a = (y * PLANE + 4 * t + c) // 4
            frame_b = frame_a + 1
            low = jnp.maximum(frame_a - win + 1, 0)
            near_count = frame_b - low + 1
            count = near_count + (sink < low).astype(jnp.int32)

            def frame_at(i):
                return jnp.where(i < near_count, low + i, sink)

            def start_of(frame):
                return jnp.clip(4 * frame - c, 0, NBLK - 4)

            q_tile = q_ref[rows]
            q_t = q_tile.T

            def scores(i, top):
                frame = frame_at(i)
                start = start_of(frame)
                see_a = sees(frame_a, frame)
                see_b = sees(frame_b, frame)
                keys = kv_ref[pl.ds(start, 4), 0].reshape(chunk, DH)
                s = jnp.dot(keys, q_t, preferred_element_type=F32)
                for k in range(4):
                    here = (start + k + c) // 4 == frame
                    bias = jnp.where(
                        lane < (4 - c) * BLK,
                        jnp.where(here & see_a, 0.0, NEG),
                        jnp.where(here & see_b, 0.0, NEG),
                    )
                    part = s[k * BLK : (k + 1) * BLK] + bias
                    t_s[pl.ds(i * chunk + k * BLK, BLK), :] = part
                    top = jnp.maximum(top, jnp.max(part.reshape(BLK // 8, 8, TILE_Q), axis=0))
                return top

            top = lax.fori_loop(0, count, scores, jnp.full((8, TILE_Q), NEG, F32))
            top = jnp.max(top, axis=0, keepdims=True) * slope

            def mix(i, carry):
                total, mixed = carry
                start = start_of(frame_at(i))
                at = pl.ds(pl.multiple_of(i * chunk, chunk), chunk)
                p = jnp.exp2(t_s[at, :] * slope - top)
                total = total + jnp.sum(p.reshape(chunk // 8, 8, TILE_Q), axis=0)
                p = p.astype(BF16)
                p_s[at, :] = p
                values = kv_ref[pl.ds(start, 4), 1].reshape(chunk, DH)
                mixed = mixed + lax.dot_general(
                    values, p, (((0,), (0,)), ((), ())), preferred_element_type=F32
                )
                return total, mixed

            total, mixed = lax.fori_loop(
                0, count, mix, (jnp.zeros((8, TILE_Q), F32), jnp.zeros((DH, TILE_Q), F32))
            )
            inverse = 1.0 / jnp.sum(total, axis=0, keepdims=True)
            att_t = (mixed * inverse).astype(BF16)
            att_ref[rows] = att_t.T
            do_t = (do_ref[rows].T.astype(F32) * inverse).astype(BF16)
            do_n = do_t.T
            delta = jnp.sum(do_t.astype(F32) * att_t.astype(F32), axis=0, keepdims=True)

            def back(i, dq_t):
                start = start_of(frame_at(i))
                at = pl.ds(pl.multiple_of(i * chunk, chunk), chunk)
                keys = kv_ref[pl.ds(start, 4), 0].reshape(chunk, DH)
                values = kv_ref[pl.ds(start, 4), 1].reshape(chunk, DH)
                p = p_s[at, :]
                dp = jnp.dot(values, do_t, preferred_element_type=F32)
                g = (p.astype(F32) * (dp - delta)).astype(BF16)
                dk = jnp.dot(g, q_tile, preferred_element_type=F32)
                dv = jnp.dot(p, do_n, preferred_element_type=F32)
                dk_s[pl.ds(start, 4)] += dk.reshape(4, BLK, DH)
                dv_s[pl.ds(start, 4)] += dv.reshape(4, BLK, DH)
                return dq_t + lax.dot_general(
                    keys, g, (((0,), (0,)), ((), ())), preferred_element_type=F32
                )

            dq_t = lax.fori_loop(0, count, back, jnp.zeros((DH, TILE_Q), F32))
            dq_ref[rows] = (dq_t * scale).astype(BF16).T

        @pl.loop(0, NBLK)
        def _(b):
            dkv_ref[b, 0] = (dk_s[b] * scale).astype(BF16)
            dkv_ref[b, 1] = dv_s[b].astype(BF16)


def scatter_kernel(
    att_ref, dq_ref, dkv_ref,
    atto_ref, dqo_ref, dko_ref, dvo_ref,
    beside, over, back, ahead, joined, done, acc,
    out_send, out_sem, done_send,
    beside_send, beside_sem, over_send, over_sem, joined_send, back_sem, ahead_send, ahead_sem,
):
    y, place, _, _ = position()
    is_owner, plane, src_head, j_there = my_task()
    sibling, across, diagonal = neighbours()
    even = plane % 2 == 0
    early = plane < 2
    late = jnp.logical_not(early)
    base = plane * PLANE
    column = pl.ds(pl.multiple_of(j_there * DH, DH), DH)

    for device in owner_ids(y):
        signal(device)

    @pl.when(is_owner)
    def _():
        signal(sibling)
        pl.when(early)(lambda: signal(across))
        pl.when(plane == 2)(lambda: signal(diagonal))
        low = (plane % 2) * PLANE
        other_low = (1 - plane % 2) * PLANE
        wait_for(jnp.where(late | (plane == 1), PLANE + 2, PLANE + 1))

        next_to = (plane + 1 - 2 * (plane % 2)) * PLANE

        @pl.when(late)
        def _():
            for r in range(PLANE):
                send(dkv_ref.at[other_low + r], over.at[r], over_send, over_sem.at[r], sibling)

        @pl.when(late)
        def _():
            for r in range(PLANE):
                settle(over.at[r], over_sem.at[r])
                joined[r] = (over[r].astype(F32) + dkv_ref[low + r].astype(F32)).astype(BF16)
                send(joined.at[r], back.at[r], joined_send, back_sem.at[r], across)

        for r in range(PLANE):
            def to_sibling(r=r):
                send(dkv_ref.at[next_to + r], beside.at[r], beside_send, beside_sem.at[r], sibling)

            if r < AHEAD:
                to_sibling()
            else:
                pl.when(jnp.logical_not(even))(to_sibling)

        @pl.when(plane == 1)
        def _():
            for r in range(AHEAD):
                send(dkv_ref.at[2 * PLANE + r], ahead.at[r], ahead_send, ahead_sem.at[r], diagonal)

        for r in range(PLANE):
            for part, (ref, out) in enumerate(((att_ref, atto_ref), (dq_ref, dqo_ref))):
                send(ref.at[pl.ds(r * BLK, BLK)], out.at[:, column], out_send.at[part],
                     out_sem.at[part], (base + r, src_head))

        for r in range(PLANE):
            acc[...] = dkv_ref[base + r].astype(F32)

            def add(buffer, sems, r=r):
                settle(buffer.at[r], sems.at[r])
                acc[...] += buffer[r].astype(F32)

            if r < AHEAD:
                add(beside, beside_sem)
                pl.when(plane == 2)(lambda add=add: add(ahead, ahead_sem))
            else:
                pl.when(even)(lambda add=add: add(beside, beside_sem))
            pl.when(early)(lambda add=add: add(back, back_sem))
            done[r] = acc[...].astype(BF16)
            for part, out in enumerate((dko_ref, dvo_ref)):
                send(done.at[r, part], out.at[:, column], done_send, out_sem.at[2 + part],
                     (base + r, src_head))
        settle(att_ref, out_send.at[0])
        settle(dq_ref, out_send.at[1])
        settle(done, done_send)
        pl.when(even)(lambda: settle(ahead, beside_send))
        pl.when(jnp.logical_not(even))(lambda: settle(done, beside_send))
        pl.when(plane == 1)(lambda: settle(ahead, ahead_send))

        @pl.when(late)
        def _():
            settle(done, over_send)
            settle(joined, joined_send)

    for part, ref in enumerate((atto_ref, dqo_ref, dko_ref, dvo_ref)):
        settle(ref, out_sem.at[part])


def finish_kernel(*refs):
    for src, out in zip(refs[:4], refs[4:]):
        out[...] = src[...]


def in_vmem(array):
    return pltpu.with_memory_space_constraint(array, pltpu.VMEM)


def in_hbm(array):
    return pltpu.with_memory_space_constraint(array, pltpu.HBM)


def per_device(query, key, value, grad_out, frame_ids, sink_frame, window):
    any_spec = pl.BlockSpec(memory_space=pl.ANY)
    smem = pl.BlockSpec(memory_space=pltpu.SMEM)
    vmem = pl.BlockSpec(memory_space=pltpu.VMEM)
    dma = pltpu.SemaphoreType.DMA
    shape = jax.ShapeDtypeStruct
    rows = PLANE * BLK
    q_all, do_all, kv_all, w_all = pl.pallas_call(
        gather_kernel,
        out_shape=(
            pltpu.VMEM((rows, DH), BF16),
            pltpu.VMEM((rows, DH), BF16),
            pltpu.VMEM((NBLK, 2, BLK, DH), BF16),
            shape((HPD,), jnp.int32),
        ),
        in_specs=[any_spec] * 5,
        out_specs=[any_spec] * 4,
        scratch_shapes=[
            dma((4,)), dma((2,)), dma((HPD,)), dma((2,)), dma((PLANE,)), dma, dma((AHEAD,)),
            dma((PLANE,)), dma((PLANE,)), dma((PLANE,)), dma, dma, dma,
        ],
        compiler_params=pltpu.CompilerParams(
            collective_id=0, has_side_effects=True, vmem_limit_bytes=8 * MIB
        ),
        name="gather",
    )(*[in_hbm(array) for array in (query, key, value, grad_out, window)])
    att, dq, dkv = pl.pallas_call(
        attend_kernel,
        out_shape=(
            pltpu.VMEM((rows, DH), BF16),
            pltpu.VMEM((rows, DH), BF16),
            pltpu.VMEM((NBLK, 2, BLK, DH), BF16),
        ),
        in_specs=[smem] * 3 + [vmem] * 3,
        out_specs=[vmem] * 3,
        scratch_shapes=[
            pltpu.VMEM((MAX_CHUNKS * 4 * BLK, TILE_Q), F32),
            pltpu.VMEM((MAX_CHUNKS * 4 * BLK, TILE_Q), BF16),
            pltpu.VMEM((NBLK, BLK, DH), F32),
            pltpu.VMEM((NBLK, BLK, DH), F32),
        ],
        compiler_params=pltpu.CompilerParams(vmem_limit_bytes=32 * MIB),
        name="attend",
    )(in_hbm(frame_ids), sink_frame, w_all, in_vmem(q_all), in_vmem(do_all), in_vmem(kv_all))

    def tiles(count):
        return pltpu.VMEM((count, 2, BLK, DH), BF16)

    outs = pl.pallas_call(
        scatter_kernel,
        out_shape=tuple(pltpu.VMEM(query.shape, BF16) for _ in range(4)),
        in_specs=[any_spec, any_spec, vmem],
        out_specs=[any_spec] * 4,
        scratch_shapes=[
            tiles(PLANE), tiles(PLANE), tiles(PLANE), tiles(AHEAD), tiles(PLANE), tiles(PLANE),
            pltpu.VMEM((2, BLK, DH), F32),
            dma((2,)), dma((4,)), dma,
            dma, dma((PLANE,)), dma, dma((PLANE,)), dma, dma((PLANE,)), dma, dma((AHEAD,)),
        ],
        compiler_params=pltpu.CompilerParams(
            collective_id=1, has_side_effects=True, vmem_limit_bytes=16 * MIB
        ),
        name="scatter",
    )(in_vmem(att), in_vmem(dq), in_vmem(dkv))
    return pl.pallas_call(
        finish_kernel,
        out_shape=tuple(shape(query.shape, BF16) for _ in range(4)),
        in_specs=[vmem] * 4,
        out_specs=[vmem] * 4,
        compiler_params=pltpu.CompilerParams(vmem_limit_bytes=8 * MIB),
        name="finish",
    )(*[in_vmem(out) for out in outs])


def solution(mesh):
    tm_head = P("tm", "head")
    return jax.shard_map(
        per_device,
        mesh=mesh,
        in_specs=(tm_head, tm_head, tm_head, tm_head, P(), P(), P("head")),
        out_specs=(tm_head, tm_head, tm_head, tm_head),
        check_vma=False,
    )
```

```python
import math

import jax
import jax.numpy as jnp
from jax import lax
from jax.experimental import pallas as pl
from jax.experimental.pallas import tpu as pltpu
from jax.sharding import PartitionSpec as P

MESH = pl.DeviceIdType.MESH
BLK = 128
DH = 128
HPD = 5
RING = 4
PLANE = 8
AHEAD = 3
NBLK = RING * PLANE
BF16 = jnp.bfloat16
F32 = jnp.float32
TILE_Q = 4 * BLK
MAX_CHUNKS = 5
NEG = -1e30
MIB = 1 << 20


def seat_of(u):
    if u < 8:
        return 2 * (u % 4) + u // 4, (u % 4 + u // 4) % 2
    return ((0, 1), (5, 0))[u - 8]


def position():
    tm = lax.axis_index("tm")
    head = lax.axis_index("head")
    return tm // PLANE, tm % PLANE, head // 2, head % 2


def owner_ids(y):
    _, _, x_lo, core = position()
    half = y // 2
    ids = []
    for j in range(HPD):
        (p0, e0), (p1, e1) = seat_of(j), seat_of(HPD + j)
        place = p0 + core * (p1 - p0)
        e = e0 + core * (e1 - e0)
        row = (1 - half) * (1 - e) + half * (2 + e)
        ids.append((row * PLANE + place, 2 * (1 - x_lo) + y % 2))
    return ids


def my_task():
    row, place, x_lo, core = position()
    half = row // 2
    e = half * (row - 2) + (1 - half) * (1 - row)
    other = (e + place // 2 + place % 2) % 2
    u = (1 - other) * (4 * (place % 2) + place // 2) + other * (8 + place // 5)
    is_owner = (other == 0) | (place == 0) | (place == 5)
    return is_owner, 2 * half + core, 2 * (1 - x_lo) + u // HPD, u % HPD


def neighbours():
    row, place, x_lo, core = position()
    tm = row * PLANE + place
    across = (RING - 1 - row) * PLANE + place
    same, swapped = 2 * x_lo + core, 2 * x_lo + 1 - core
    return (tm, swapped), (across, same), (across, swapped)


def in_order(place, steps):
    return [(place // 2 * 2 + 2 * step + i) % PLANE for step in steps for i in range(2)]


def signal(device):
    pl.semaphore_signal(
        pltpu.get_barrier_semaphore(), inc=1, device_id=device, device_id_type=MESH
    )


def wait_for(count):
    pl.semaphore_wait(pltpu.get_barrier_semaphore(), count)


def send(src, dst, send_sem, recv_sem, device):
    pltpu.make_async_remote_copy(
        src_ref=src, dst_ref=dst, send_sem=send_sem, recv_sem=recv_sem,
        device_id=device, device_id_type=MESH,
    ).start()


def settle(ref, sem):
    pltpu.make_async_copy(ref, ref, sem).wait()


def gather_kernel(
    q_ref, k_ref, v_ref, do_ref, w_ref,
    qo_ref, doo_ref, kvo_ref, wo_ref,
    send_sem, ahead_send, w_send, qd_sem, kv_sem, w_sem, ahead_sem,
    sib_sem, cross_sem, relay_sem, sib_send, cross_send, relay_send,
):
    y, place, _, _ = position()
    is_owner, plane, src_head, _ = my_task()
    sibling, across, _ = neighbours()
    even = plane % 2 == 0
    early = plane < 2
    looked_at = (y == 2) & (place < AHEAD)

    @pl.when(is_owner)
    def _():
        for r in range(PLANE):
            signal((plane * PLANE + r, src_head))
        signal(sibling)
        pl.when(jnp.logical_not(early))(lambda: signal(across))

        @pl.when(plane == 1)
        def _():
            for r in range(AHEAD):
                signal((2 * PLANE + r, src_head))

    wait_for(
        jnp.where(looked_at, 2 * HPD, HPD)
        + jnp.where(is_owner, 1, 0)
        + jnp.where(is_owner & early, 1, 0)
    )

    def column(ref, j):
        return ref.at[:, pl.ds(j * DH, DH)]

    rows = pl.ds(pl.multiple_of(place * BLK, BLK), BLK)
    targets = owner_ids(y)
    tile = y * PLANE + place
    for j in range(HPD):
        for part, ref in enumerate((k_ref, v_ref)):
            send(column(ref, j), kvo_ref.at[tile, part], send_sem.at[part], kv_sem.at[place],
                 targets[j])

    @pl.when(looked_at)
    def _():
        for j, device in enumerate(owner_ids(1)):
            for part, ref in enumerate((k_ref, v_ref)):
                send(column(ref, j), kvo_ref.at[tile, part], ahead_send.at[part],
                     ahead_sem.at[place], device)

    for j in range(HPD):
        for part, (ref, out) in enumerate(((q_ref, qo_ref), (do_ref, doo_ref))):
            send(column(ref, j), out.at[rows], send_sem.at[2 + part], qd_sem.at[part], targets[j])

    @pl.when(place == 0)
    def _():
        for j in range(HPD):
            send(w_ref, wo_ref, w_send.at[j], w_sem, targets[j])

    @pl.when(is_owner)
    def _():
        base = plane * PLANE

        def pass_on(block, to, recv, sent):
            send(kvo_ref.at[block], kvo_ref.at[block], sent, recv, to)

        nearest_first = in_order(place, (0, 1, 3, 2))
        for r in nearest_first:
            settle(kvo_ref.at[base + r], kv_sem.at[r])
            pl.when(early)(lambda r=r: pass_on(base + r, across, cross_sem.at[r], cross_send))
            pl.when(even | (r < AHEAD))(
                lambda r=r: pass_on(base + r, sibling, sib_sem.at[r], sib_send)
            )

        @pl.when(jnp.logical_not(early))
        def _():
            mine = (plane - 2) * PLANE
            theirs = (1 - (plane - 2)) * PLANE
            for r in nearest_first:
                settle(kvo_ref.at[mine + r], cross_sem.at[r])
                pass_on(mine + r, sibling, relay_sem.at[r], relay_send)
            for r in range(PLANE):
                settle(kvo_ref.at[theirs + r], relay_sem.at[r])
            settle(kvo_ref.at[pl.ds(0, PLANE)], relay_send)

        beside = (plane + 1 - 2 * (plane % 2)) * PLANE
        for r in range(AHEAD):
            settle(kvo_ref.at[beside + r], sib_sem.at[r])

        @pl.when(jnp.logical_not(even))
        def _():
            for r in range(AHEAD, PLANE):
                settle(kvo_ref.at[beside + r], sib_sem.at[r])

        @pl.when(plane == 1)
        def _():
            for r in range(AHEAD):
                settle(kvo_ref.at[2 * PLANE + r], ahead_sem.at[r])

        settle(qo_ref, qd_sem.at[0])
        settle(doo_ref, qd_sem.at[1])
        settle(wo_ref, w_sem)
        pl.when(early)(lambda: settle(kvo_ref.at[pl.ds(0, PLANE)], cross_send))
        pl.when(even)(lambda: settle(kvo_ref.at[pl.ds(0, PLANE)], sib_send))
        pl.when(jnp.logical_not(even))(
            lambda: settle(kvo_ref.at[pl.ds(0, AHEAD)], sib_send)
        )

    for part, ref in enumerate((k_ref, v_ref, q_ref, do_ref)):
        settle(ref, send_sem.at[part])

    @pl.when(looked_at)
    def _():
        settle(k_ref, ahead_send.at[0])
        settle(v_ref, ahead_send.at[1])

    @pl.when(place == 0)
    def _():
        for j in range(HPD):
            settle(w_ref, w_send.at[j])


def attend_kernel(
    fid_ref, sink_ref, w_ref, q_ref, do_ref, kv_ref,
    att_ref, dq_ref, dkv_ref,
    t_s, p_s, dk_s, dv_s,
):
    is_owner, y, _, src_j = my_task()
    scale = 1.0 / math.sqrt(DH)
    slope = scale * math.log2(math.e)
    chunk = 4 * BLK

    @pl.when(is_owner)
    def _():
        c = 1 + fid_ref[1] + fid_ref[2]
        sink = sink_ref[0]
        win = w_ref[src_j]
        dk_s[...] = jnp.zeros_like(dk_s)
        dv_s[...] = jnp.zeros_like(dv_s)
        lane = lax.broadcasted_iota(jnp.int32, (1, TILE_Q), 1)

        def sees(query_frame, frame):
            near = (frame <= query_frame) & (frame > query_frame - win)
            return near | ((frame == sink) & (sink <= query_frame))

        @pl.loop(0, PLANE // 4)
        def _(t):
            rows = pl.ds(pl.multiple_of(t * TILE_Q, TILE_Q), TILE_Q)
            frame_a = (y * PLANE + 4 * t + c) // 4
            frame_b = frame_a + 1
            low = jnp.maximum(frame_a - win + 1, 0)
            near_count = frame_b - low + 1
            count = near_count + (sink < low).astype(jnp.int32)

            def frame_at(i):
                return jnp.where(i < near_count, low + i, sink)

            def start_of(frame):
                return jnp.clip(4 * frame - c, 0, NBLK - 4)

            q_tile = q_ref[rows]
            q_t = q_tile.T

            def scores(i, top):
                frame = frame_at(i)
                start = start_of(frame)
                see_a = sees(frame_a, frame)
                see_b = sees(frame_b, frame)
                keys = kv_ref[pl.ds(start, 4), 0].reshape(chunk, DH)
                s = jnp.dot(keys, q_t, preferred_element_type=F32)
                for k in range(4):
                    here = (start + k + c) // 4 == frame
                    bias = jnp.where(
                        lane < (4 - c) * BLK,
                        jnp.where(here & see_a, 0.0, NEG),
                        jnp.where(here & see_b, 0.0, NEG),
                    )
                    part = s[k * BLK : (k + 1) * BLK] + bias
                    t_s[pl.ds(i * chunk + k * BLK, BLK), :] = part
                    top = jnp.maximum(top, jnp.max(part.reshape(BLK // 8, 8, TILE_Q), axis=0))
                return top

            top = lax.fori_loop(0, count, scores, jnp.full((8, TILE_Q), NEG, F32))
            top = jnp.max(top, axis=0, keepdims=True) * slope

            def mix(i, carry):
                total, mixed = carry
                start = start_of(frame_at(i))
                at = pl.ds(pl.multiple_of(i * chunk, chunk), chunk)
                p = jnp.exp2(t_s[at, :] * slope - top)
                total = total + jnp.sum(p.reshape(chunk // 8, 8, TILE_Q), axis=0)
                p = p.astype(BF16)
                p_s[at, :] = p
                values = kv_ref[pl.ds(start, 4), 1].reshape(chunk, DH)
                mixed = mixed + lax.dot_general(
                    values, p, (((0,), (0,)), ((), ())), preferred_element_type=F32
                )
                return total, mixed

            total, mixed = lax.fori_loop(
                0, count, mix, (jnp.zeros((8, TILE_Q), F32), jnp.zeros((DH, TILE_Q), F32))
            )
            inverse = 1.0 / jnp.sum(total, axis=0, keepdims=True)
            att_t = (mixed * inverse).astype(BF16)
            att_ref[rows] = att_t.T
            do_t = (do_ref[rows].T.astype(F32) * inverse).astype(BF16)
            do_n = do_t.T
            delta = jnp.sum(do_t.astype(F32) * att_t.astype(F32), axis=0, keepdims=True)

            def back(i, dq_t):
                start = start_of(frame_at(i))
                at = pl.ds(pl.multiple_of(i * chunk, chunk), chunk)
                keys = kv_ref[pl.ds(start, 4), 0].reshape(chunk, DH)
                values = kv_ref[pl.ds(start, 4), 1].reshape(chunk, DH)
                p = p_s[at, :]
                dp = jnp.dot(values, do_t, preferred_element_type=F32)
                g = (p.astype(F32) * (dp - delta)).astype(BF16)
                dk = jnp.dot(g, q_tile, preferred_element_type=F32)
                dv = jnp.dot(p, do_n, preferred_element_type=F32)
                dk_s[pl.ds(start, 4)] += dk.reshape(4, BLK, DH)
                dv_s[pl.ds(start, 4)] += dv.reshape(4, BLK, DH)
                return dq_t + lax.dot_general(
                    keys, g, (((0,), (0,)), ((), ())), preferred_element_type=F32
                )

            dq_t = lax.fori_loop(0, count, back, jnp.zeros((DH, TILE_Q), F32))
            dq_ref[rows] = (dq_t * scale).astype(BF16).T

        @pl.loop(0, NBLK)
        def _(b):
            dkv_ref[b, 0] = (dk_s[b] * scale).astype(BF16)
            dkv_ref[b, 1] = dv_s[b].astype(BF16)


def scatter_kernel(
    att_ref, dq_ref, dkv_ref,
    atto_ref, dqo_ref, dko_ref, dvo_ref,
    beside, over, back, ahead, joined, done, acc,
    out_send, out_sem, done_send,
    beside_send, beside_sem, over_send, over_sem, joined_send, back_sem, ahead_send, ahead_sem,
):
    y, place, _, _ = position()
    is_owner, plane, src_head, j_there = my_task()
    sibling, across, diagonal = neighbours()
    even = plane % 2 == 0
    early = plane < 2
    late = jnp.logical_not(early)
    base = plane * PLANE
    column = pl.ds(pl.multiple_of(j_there * DH, DH), DH)

    for device in owner_ids(y):
        signal(device)

    @pl.when(is_owner)
    def _():
        signal(sibling)
        pl.when(early)(lambda: signal(across))
        pl.when(plane == 2)(lambda: signal(diagonal))
        low = (plane % 2) * PLANE
        other_low = (1 - plane % 2) * PLANE
        wait_for(jnp.where(late | (plane == 1), PLANE + 2, PLANE + 1))

        next_to = (plane + 1 - 2 * (plane % 2)) * PLANE
        farthest_first = in_order(place, (2, 1, 3, 0))

        @pl.when(late)
        def _():
            for r in farthest_first:
                send(dkv_ref.at[other_low + r], over.at[r], over_send, over_sem.at[r], sibling)

        @pl.when(late)
        def _():
            for r in farthest_first:
                settle(over.at[r], over_sem.at[r])
                joined[r] = (over[r].astype(F32) + dkv_ref[low + r].astype(F32)).astype(BF16)
                send(joined.at[r], back.at[r], joined_send, back_sem.at[r], across)

        for r in farthest_first:
            def to_sibling(r=r):
                send(dkv_ref.at[next_to + r], beside.at[r], beside_send, beside_sem.at[r], sibling)

            pl.when(jnp.logical_not(even) | (r < AHEAD))(to_sibling)

        @pl.when(plane == 1)
        def _():
            for r in range(AHEAD):
                send(dkv_ref.at[2 * PLANE + r], ahead.at[r], ahead_send, ahead_sem.at[r], diagonal)

        for r in farthest_first:
            for part, (ref, out) in enumerate(((att_ref, atto_ref), (dq_ref, dqo_ref))):
                send(ref.at[pl.ds(pl.multiple_of(r * BLK, BLK), BLK)], out.at[:, column], out_send.at[part],
                     out_sem.at[part], (base + r, src_head))

        for r in farthest_first:
            acc[...] = dkv_ref[base + r].astype(F32)

            def add(buffer, sems, r=r):
                settle(buffer.at[r], sems.at[r])
                acc[...] += buffer[r].astype(F32)

            pl.when(even | (r < AHEAD))(lambda add=add: add(beside, beside_sem))
            pl.when((plane == 2) & (r < AHEAD))(lambda add=add: add(ahead, ahead_sem))
            pl.when(early)(lambda add=add: add(back, back_sem))
            done[r] = acc[...].astype(BF16)
            for part, out in enumerate((dko_ref, dvo_ref)):
                send(done.at[r, part], out.at[:, column], done_send, out_sem.at[2 + part],
                     (base + r, src_head))
        settle(att_ref, out_send.at[0])
        settle(dq_ref, out_send.at[1])
        settle(done, done_send)
        pl.when(even)(lambda: settle(ahead, beside_send))
        pl.when(jnp.logical_not(even))(lambda: settle(done, beside_send))
        pl.when(plane == 1)(lambda: settle(ahead, ahead_send))

        @pl.when(late)
        def _():
            settle(done, over_send)
            settle(joined, joined_send)

    for part, ref in enumerate((atto_ref, dqo_ref, dko_ref, dvo_ref)):
        settle(ref, out_sem.at[part])


def finish_kernel(*refs):
    for src, out in zip(refs[:4], refs[4:]):
        out[...] = src[...]


def in_vmem(array):
    return pltpu.with_memory_space_constraint(array, pltpu.VMEM)


def in_hbm(array):
    return pltpu.with_memory_space_constraint(array, pltpu.HBM)


def per_device(query, key, value, grad_out, frame_ids, sink_frame, window):
    any_spec = pl.BlockSpec(memory_space=pl.ANY)
    smem = pl.BlockSpec(memory_space=pltpu.SMEM)
    vmem = pl.BlockSpec(memory_space=pltpu.VMEM)
    dma = pltpu.SemaphoreType.DMA
    shape = jax.ShapeDtypeStruct
    rows = PLANE * BLK
    q_all, do_all, kv_all, w_all = pl.pallas_call(
        gather_kernel,
        out_shape=(
            pltpu.VMEM((rows, DH), BF16),
            pltpu.VMEM((rows, DH), BF16),
            pltpu.VMEM((NBLK, 2, BLK, DH), BF16),
            shape((HPD,), jnp.int32),
        ),
        in_specs=[any_spec] * 5,
        out_specs=[any_spec] * 4,
        scratch_shapes=[
            dma((4,)), dma((2,)), dma((HPD,)), dma((2,)), dma((PLANE,)), dma, dma((AHEAD,)),
            dma((PLANE,)), dma((PLANE,)), dma((PLANE,)), dma, dma, dma,
        ],
        compiler_params=pltpu.CompilerParams(
            collective_id=0, has_side_effects=True, vmem_limit_bytes=8 * MIB
        ),
        name="gather",
    )(*[in_hbm(array) for array in (query, key, value, grad_out, window)])
    att, dq, dkv = pl.pallas_call(
        attend_kernel,
        out_shape=(
            pltpu.VMEM((rows, DH), BF16),
            pltpu.VMEM((rows, DH), BF16),
            pltpu.VMEM((NBLK, 2, BLK, DH), BF16),
        ),
        in_specs=[smem] * 3 + [vmem] * 3,
        out_specs=[vmem] * 3,
        scratch_shapes=[
            pltpu.VMEM((MAX_CHUNKS * 4 * BLK, TILE_Q), F32),
            pltpu.VMEM((MAX_CHUNKS * 4 * BLK, TILE_Q), BF16),
            pltpu.VMEM((NBLK, BLK, DH), F32),
            pltpu.VMEM((NBLK, BLK, DH), F32),
        ],
        compiler_params=pltpu.CompilerParams(vmem_limit_bytes=32 * MIB),
        name="attend",
    )(in_hbm(frame_ids), sink_frame, w_all, in_vmem(q_all), in_vmem(do_all), in_vmem(kv_all))

    def tiles(count):
        return pltpu.VMEM((count, 2, BLK, DH), BF16)

    outs = pl.pallas_call(
        scatter_kernel,
        out_shape=tuple(pltpu.VMEM(query.shape, BF16) for _ in range(4)),
        in_specs=[any_spec, any_spec, vmem],
        out_specs=[any_spec] * 4,
        scratch_shapes=[
            tiles(PLANE), tiles(PLANE), tiles(PLANE), tiles(AHEAD), tiles(PLANE), tiles(PLANE),
            pltpu.VMEM((2, BLK, DH), F32),
            dma((2,)), dma((4,)), dma,
            dma, dma((PLANE,)), dma, dma((PLANE,)), dma, dma((PLANE,)), dma, dma((AHEAD,)),
        ],
        compiler_params=pltpu.CompilerParams(
            collective_id=1, has_side_effects=True, vmem_limit_bytes=16 * MIB
        ),
        name="scatter",
    )(in_vmem(att), in_vmem(dq), in_vmem(dkv))
    return pl.pallas_call(
        finish_kernel,
        out_shape=tuple(shape(query.shape, BF16) for _ in range(4)),
        in_specs=[vmem] * 4,
        out_specs=[vmem] * 4,
        compiler_params=pltpu.CompilerParams(vmem_limit_bytes=8 * MIB),
        name="finish",
    )(*[in_vmem(out) for out in outs])


def solution(mesh):
    tm_head = P("tm", "head")
    return jax.shard_map(
        per_device,
        mesh=mesh,
        in_specs=(tm_head, tm_head, tm_head, tm_head, P(), P(), P("head")),
        out_specs=(tm_head, tm_head, tm_head, tm_head),
        check_vma=False,
    )
```

```python
import math

import jax
import jax.numpy as jnp
from jax import lax
from jax.experimental import pallas as pl
from jax.experimental.pallas import tpu as pltpu
from jax.sharding import PartitionSpec as P

MESH = pl.DeviceIdType.MESH
BLK = 128
DH = 128
HPD = 5
RING = 4
PLANE = 8
AHEAD = 3
NBLK = RING * PLANE
BF16 = jnp.bfloat16
F32 = jnp.float32
TILE_Q = 4 * BLK
MAX_CHUNKS = 5
NEG = -1e30
MIB = 1 << 20


def seat_of(u):
    if u < 8:
        return 2 * (u % 4) + u // 4, (u % 4 + u // 4) % 2
    return ((0, 1), (5, 0))[u - 8]


def position():
    tm = lax.axis_index("tm")
    head = lax.axis_index("head")
    return tm // PLANE, tm % PLANE, head // 2, head % 2


def owner_ids(y):
    _, _, x_lo, core = position()
    half = y // 2
    ids = []
    for j in range(HPD):
        (p0, e0), (p1, e1) = seat_of(j), seat_of(HPD + j)
        place = p0 + core * (p1 - p0)
        e = e0 + core * (e1 - e0)
        row = (1 - half) * (1 - e) + half * (2 + e)
        ids.append((row * PLANE + place, 2 * (1 - x_lo) + y % 2))
    return ids


def my_task():
    row, place, x_lo, core = position()
    half = row // 2
    e = half * (row - 2) + (1 - half) * (1 - row)
    other = (e + place // 2 + place % 2) % 2
    u = (1 - other) * (4 * (place % 2) + place // 2) + other * (8 + place // 5)
    is_owner = (other == 0) | (place == 0) | (place == 5)
    return is_owner, 2 * half + core, 2 * (1 - x_lo) + u // HPD, u % HPD


def neighbours():
    row, place, x_lo, core = position()
    tm = row * PLANE + place
    across = (RING - 1 - row) * PLANE + place
    same, swapped = 2 * x_lo + core, 2 * x_lo + 1 - core
    return (tm, swapped), (across, same), (across, swapped)


def in_order(place, steps):
    return [(place // 2 * 2 + 2 * step + i) % PLANE for step in steps for i in range(2)]


def signal(device):
    pl.semaphore_signal(
        pltpu.get_barrier_semaphore(), inc=1, device_id=device, device_id_type=MESH
    )


def wait_for(count):
    pl.semaphore_wait(pltpu.get_barrier_semaphore(), count)


def send(src, dst, send_sem, recv_sem, device):
    pltpu.make_async_remote_copy(
        src_ref=src, dst_ref=dst, send_sem=send_sem, recv_sem=recv_sem,
        device_id=device, device_id_type=MESH,
    ).start()


def settle(ref, sem):
    pltpu.make_async_copy(ref, ref, sem).wait()


def gather_kernel(
    q_ref, k_ref, v_ref, do_ref, w_ref,
    qo_ref, doo_ref, kvo_ref, wo_ref,
    send_sem, ahead_send, w_send, qd_sem, kv_sem, w_sem, ahead_sem,
    sib_sem, cross_sem, relay_sem, sib_send, cross_send, relay_send,
):
    y, place, _, _ = position()
    is_owner, plane, src_head, _ = my_task()
    sibling, across, _ = neighbours()
    even = plane % 2 == 0
    early = plane < 2
    looked_at = (y == 2) & (place < AHEAD)

    @pl.when(is_owner)
    def _():
        for r in range(PLANE):
            signal((plane * PLANE + r, src_head))
        signal(sibling)
        pl.when(jnp.logical_not(early))(lambda: signal(across))

        @pl.when(plane == 1)
        def _():
            for r in range(AHEAD):
                signal((2 * PLANE + r, src_head))

    wait_for(
        jnp.where(looked_at, 2 * HPD, HPD)
        + jnp.where(is_owner, 1, 0)
        + jnp.where(is_owner & early, 1, 0)
    )

    def column(ref, j):
        return ref.at[:, pl.ds(j * DH, DH)]

    rows = pl.ds(pl.multiple_of(place * BLK, BLK), BLK)
    targets = owner_ids(y)
    tile = y * PLANE + place
    for j in range(HPD):
        for part, ref in enumerate((k_ref, v_ref)):
            send(column(ref, j), kvo_ref.at[tile, part], send_sem.at[part], kv_sem.at[place],
                 targets[j])

    @pl.when(looked_at)
    def _():
        for j, device in enumerate(owner_ids(1)):
            for part, ref in enumerate((k_ref, v_ref)):
                send(column(ref, j), kvo_ref.at[tile, part], ahead_send.at[part],
                     ahead_sem.at[place], device)

    for j in range(HPD):
        for part, (ref, out) in enumerate(((q_ref, qo_ref), (do_ref, doo_ref))):
            send(column(ref, j), out.at[rows], send_sem.at[2 + part], qd_sem.at[part], targets[j])

    @pl.when(place == 0)
    def _():
        for j in range(HPD):
            send(w_ref, wo_ref, w_send.at[j], w_sem, targets[j])

    @pl.when(is_owner)
    def _():
        base = plane * PLANE

        def pass_on(block, to, recv, sent):
            send(kvo_ref.at[block], kvo_ref.at[block], sent, recv, to)

        nearest_first = in_order(place, (0, 1, 3, 2))
        mine = plane % 2 * PLANE
        for r in nearest_first:
            settle(kvo_ref.at[base + r], kv_sem.at[r])
            pl.when(early)(lambda r=r: pass_on(base + r, across, cross_sem.at[r], cross_send))
            pl.when(even | (r < AHEAD))(
                lambda r=r: pass_on(base + r, sibling, sib_sem.at[r], sib_send)
            )

            @pl.when(jnp.logical_not(early))
            def _(r=r):
                settle(kvo_ref.at[mine + r], cross_sem.at[r])
                pass_on(mine + r, sibling, relay_sem.at[r], relay_send)

        @pl.when(jnp.logical_not(early))
        def _():
            theirs = (1 - (plane - 2)) * PLANE
            for r in range(PLANE):
                settle(kvo_ref.at[theirs + r], relay_sem.at[r])
            settle(kvo_ref.at[pl.ds(0, PLANE)], relay_send)

        beside = (plane + 1 - 2 * (plane % 2)) * PLANE
        for r in range(AHEAD):
            settle(kvo_ref.at[beside + r], sib_sem.at[r])

        @pl.when(jnp.logical_not(even))
        def _():
            for r in range(AHEAD, PLANE):
                settle(kvo_ref.at[beside + r], sib_sem.at[r])

        @pl.when(plane == 1)
        def _():
            for r in range(AHEAD):
                settle(kvo_ref.at[2 * PLANE + r], ahead_sem.at[r])

        settle(qo_ref, qd_sem.at[0])
        settle(doo_ref, qd_sem.at[1])
        settle(wo_ref, w_sem)
        pl.when(early)(lambda: settle(kvo_ref.at[pl.ds(0, PLANE)], cross_send))
        pl.when(even)(lambda: settle(kvo_ref.at[pl.ds(0, PLANE)], sib_send))
        pl.when(jnp.logical_not(even))(
            lambda: settle(kvo_ref.at[pl.ds(0, AHEAD)], sib_send)
        )

    for part, ref in enumerate((k_ref, v_ref, q_ref, do_ref)):
        settle(ref, send_sem.at[part])

    @pl.when(looked_at)
    def _():
        settle(k_ref, ahead_send.at[0])
        settle(v_ref, ahead_send.at[1])

    @pl.when(place == 0)
    def _():
        for j in range(HPD):
            settle(w_ref, w_send.at[j])


def attend_kernel(
    fid_ref, sink_ref, w_ref, q_ref, do_ref, kv_ref,
    att_ref, dq_ref, dkv_ref,
    t_s, p_s, dk_s, dv_s,
):
    is_owner, y, _, src_j = my_task()
    scale = 1.0 / math.sqrt(DH)
    slope = scale * math.log2(math.e)
    chunk = 4 * BLK

    @pl.when(is_owner)
    def _():
        c = 1 + fid_ref[1] + fid_ref[2]
        sink = sink_ref[0]
        win = w_ref[src_j]
        dk_s[...] = jnp.zeros_like(dk_s)
        dv_s[...] = jnp.zeros_like(dv_s)
        lane = lax.broadcasted_iota(jnp.int32, (1, TILE_Q), 1)

        def sees(query_frame, frame):
            near = (frame <= query_frame) & (frame > query_frame - win)
            return near | ((frame == sink) & (sink <= query_frame))

        @pl.loop(0, PLANE // 4)
        def _(t):
            rows = pl.ds(pl.multiple_of(t * TILE_Q, TILE_Q), TILE_Q)
            frame_a = (y * PLANE + 4 * t + c) // 4
            frame_b = frame_a + 1
            low = jnp.maximum(frame_a - win + 1, 0)
            near_count = frame_b - low + 1
            count = near_count + (sink < low).astype(jnp.int32)

            def frame_at(i):
                return jnp.where(i < near_count, low + i, sink)

            def start_of(frame):
                return jnp.clip(4 * frame - c, 0, NBLK - 4)

            q_tile = q_ref[rows]
            q_t = q_tile.T

            def scores(i, top):
                frame = frame_at(i)
                start = start_of(frame)
                see_a = sees(frame_a, frame)
                see_b = sees(frame_b, frame)
                keys = kv_ref[pl.ds(start, 4), 0].reshape(chunk, DH)
                s = jnp.dot(keys, q_t, preferred_element_type=F32)
                for k in range(4):
                    here = (start + k + c) // 4 == frame
                    bias = jnp.where(
                        lane < (4 - c) * BLK,
                        jnp.where(here & see_a, 0.0, NEG),
                        jnp.where(here & see_b, 0.0, NEG),
                    )
                    part = s[k * BLK : (k + 1) * BLK] + bias
                    t_s[pl.ds(i * chunk + k * BLK, BLK), :] = part
                    top = jnp.maximum(top, jnp.max(part.reshape(BLK // 8, 8, TILE_Q), axis=0))
                return top

            top = lax.fori_loop(0, count, scores, jnp.full((8, TILE_Q), NEG, F32))
            top = jnp.max(top, axis=0, keepdims=True) * slope

            def mix(i, carry):
                total, mixed = carry
                start = start_of(frame_at(i))
                at = pl.ds(pl.multiple_of(i * chunk, chunk), chunk)
                p = jnp.exp2(t_s[at, :] * slope - top)
                total = total + jnp.sum(p.reshape(chunk // 8, 8, TILE_Q), axis=0)
                p = p.astype(BF16)
                p_s[at, :] = p
                values = kv_ref[pl.ds(start, 4), 1].reshape(chunk, DH)
                mixed = mixed + lax.dot_general(
                    values, p, (((0,), (0,)), ((), ())), preferred_element_type=F32
                )
                return total, mixed

            total, mixed = lax.fori_loop(
                0, count, mix, (jnp.zeros((8, TILE_Q), F32), jnp.zeros((DH, TILE_Q), F32))
            )
            inverse = 1.0 / jnp.sum(total, axis=0, keepdims=True)
            att_t = (mixed * inverse).astype(BF16)
            att_ref[rows] = att_t.T
            do_t = (do_ref[rows].T.astype(F32) * inverse).astype(BF16)
            do_n = do_t.T
            delta = jnp.sum(do_t.astype(F32) * att_t.astype(F32), axis=0, keepdims=True)

            def back(i, dq_t):
                start = start_of(frame_at(i))
                at = pl.ds(pl.multiple_of(i * chunk, chunk), chunk)
                keys = kv_ref[pl.ds(start, 4), 0].reshape(chunk, DH)
                values = kv_ref[pl.ds(start, 4), 1].reshape(chunk, DH)
                p = p_s[at, :]
                dp = jnp.dot(values, do_t, preferred_element_type=F32)
                g = (p.astype(F32) * (dp - delta)).astype(BF16)
                dk = jnp.dot(g, q_tile, preferred_element_type=F32)
                dv = jnp.dot(p, do_n, preferred_element_type=F32)
                dk_s[pl.ds(start, 4)] += dk.reshape(4, BLK, DH)
                dv_s[pl.ds(start, 4)] += dv.reshape(4, BLK, DH)
                return dq_t + lax.dot_general(
                    keys, g, (((0,), (0,)), ((), ())), preferred_element_type=F32
                )

            dq_t = lax.fori_loop(0, count, back, jnp.zeros((DH, TILE_Q), F32))
            dq_ref[rows] = (dq_t * scale).astype(BF16).T

        @pl.loop(0, NBLK)
        def _(b):
            dkv_ref[b, 0] = (dk_s[b] * scale).astype(BF16)
            dkv_ref[b, 1] = dv_s[b].astype(BF16)


def scatter_kernel(
    att_ref, dq_ref, dkv_ref,
    atto_ref, dqo_ref, dko_ref, dvo_ref,
    beside, over, back, ahead, joined, done, acc,
    out_send, out_sem, done_send,
    beside_send, beside_sem, over_send, over_sem, joined_send, back_sem, ahead_send, ahead_sem,
):
    y, place, _, _ = position()
    is_owner, plane, src_head, j_there = my_task()
    sibling, across, diagonal = neighbours()
    even = plane % 2 == 0
    early = plane < 2
    late = jnp.logical_not(early)
    base = plane * PLANE
    column = pl.ds(pl.multiple_of(j_there * DH, DH), DH)

    for device in owner_ids(y):
        signal(device)

    @pl.when(is_owner)
    def _():
        signal(sibling)
        pl.when(early)(lambda: signal(across))
        pl.when(plane == 2)(lambda: signal(diagonal))
        low = (plane % 2) * PLANE
        other_low = (1 - plane % 2) * PLANE
        wait_for(jnp.where(late | (plane == 1), PLANE + 2, PLANE + 1))

        next_to = (plane + 1 - 2 * (plane % 2)) * PLANE
        farthest_first = in_order(place, (2, 1, 3, 0))

        @pl.when(late)
        def _():
            for r in farthest_first:
                send(dkv_ref.at[other_low + r], over.at[r], over_send, over_sem.at[r], sibling)

        @pl.when(late)
        def _():
            for r in farthest_first:
                settle(over.at[r], over_sem.at[r])
                joined[r] = (over[r].astype(F32) + dkv_ref[low + r].astype(F32)).astype(BF16)
                send(joined.at[r], back.at[r], joined_send, back_sem.at[r], across)

        for r in farthest_first:
            def to_sibling(r=r):
                send(dkv_ref.at[next_to + r], beside.at[r], beside_send, beside_sem.at[r], sibling)

            pl.when(jnp.logical_not(even) | (r < AHEAD))(to_sibling)

        @pl.when(plane == 1)
        def _():
            for r in range(AHEAD):
                send(dkv_ref.at[2 * PLANE + r], ahead.at[r], ahead_send, ahead_sem.at[r], diagonal)

        for r in farthest_first:
            for part, (ref, out) in enumerate(((att_ref, atto_ref), (dq_ref, dqo_ref))):
                send(ref.at[pl.ds(pl.multiple_of(r * BLK, BLK), BLK)], out.at[:, column], out_send.at[part],
                     out_sem.at[part], (base + r, src_head))

        for r in farthest_first:
            acc[...] = dkv_ref[base + r].astype(F32)

            def add(buffer, sems, r=r):
                settle(buffer.at[r], sems.at[r])
                acc[...] += buffer[r].astype(F32)

            pl.when(even | (r < AHEAD))(lambda add=add: add(beside, beside_sem))
            pl.when((plane == 2) & (r < AHEAD))(lambda add=add: add(ahead, ahead_sem))
            pl.when(early)(lambda add=add: add(back, back_sem))
            done[r] = acc[...].astype(BF16)
            for part, out in enumerate((dko_ref, dvo_ref)):
                send(done.at[r, part], out.at[:, column], done_send, out_sem.at[2 + part],
                     (base + r, src_head))
        settle(att_ref, out_send.at[0])
        settle(dq_ref, out_send.at[1])
        settle(done, done_send)
        pl.when(even)(lambda: settle(ahead, beside_send))
        pl.when(jnp.logical_not(even))(lambda: settle(done, beside_send))
        pl.when(plane == 1)(lambda: settle(ahead, ahead_send))

        @pl.when(late)
        def _():
            settle(done, over_send)
            settle(joined, joined_send)

    for part, ref in enumerate((atto_ref, dqo_ref, dko_ref, dvo_ref)):
        settle(ref, out_sem.at[part])


def finish_kernel(*refs):
    for src, out in zip(refs[:4], refs[4:]):
        out[...] = src[...]


def in_vmem(array):
    return pltpu.with_memory_space_constraint(array, pltpu.VMEM)


def in_hbm(array):
    return pltpu.with_memory_space_constraint(array, pltpu.HBM)


def per_device(query, key, value, grad_out, frame_ids, sink_frame, window):
    any_spec = pl.BlockSpec(memory_space=pl.ANY)
    smem = pl.BlockSpec(memory_space=pltpu.SMEM)
    vmem = pl.BlockSpec(memory_space=pltpu.VMEM)
    dma = pltpu.SemaphoreType.DMA
    shape = jax.ShapeDtypeStruct
    rows = PLANE * BLK
    q_all, do_all, kv_all, w_all = pl.pallas_call(
        gather_kernel,
        out_shape=(
            pltpu.VMEM((rows, DH), BF16),
            pltpu.VMEM((rows, DH), BF16),
            pltpu.VMEM((NBLK, 2, BLK, DH), BF16),
            shape((HPD,), jnp.int32),
        ),
        in_specs=[any_spec] * 5,
        out_specs=[any_spec] * 4,
        scratch_shapes=[
            dma((4,)), dma((2,)), dma((HPD,)), dma((2,)), dma((PLANE,)), dma, dma((AHEAD,)),
            dma((PLANE,)), dma((PLANE,)), dma((PLANE,)), dma, dma, dma,
        ],
        compiler_params=pltpu.CompilerParams(
            collective_id=0, has_side_effects=True, vmem_limit_bytes=8 * MIB
        ),
        name="gather",
    )(*[in_hbm(array) for array in (query, key, value, grad_out, window)])
    att, dq, dkv = pl.pallas_call(
        attend_kernel,
        out_shape=(
            pltpu.VMEM((rows, DH), BF16),
            pltpu.VMEM((rows, DH), BF16),
            pltpu.VMEM((NBLK, 2, BLK, DH), BF16),
        ),
        in_specs=[smem] * 3 + [vmem] * 3,
        out_specs=[vmem] * 3,
        scratch_shapes=[
            pltpu.VMEM((MAX_CHUNKS * 4 * BLK, TILE_Q), F32),
            pltpu.VMEM((MAX_CHUNKS * 4 * BLK, TILE_Q), BF16),
            pltpu.VMEM((NBLK, BLK, DH), F32),
            pltpu.VMEM((NBLK, BLK, DH), F32),
        ],
        compiler_params=pltpu.CompilerParams(vmem_limit_bytes=32 * MIB),
        name="attend",
    )(in_hbm(frame_ids), sink_frame, w_all, in_vmem(q_all), in_vmem(do_all), in_vmem(kv_all))

    def tiles(count):
        return pltpu.VMEM((count, 2, BLK, DH), BF16)

    outs = pl.pallas_call(
        scatter_kernel,
        out_shape=tuple(pltpu.VMEM(query.shape, BF16) for _ in range(4)),
        in_specs=[any_spec, any_spec, vmem],
        out_specs=[any_spec] * 4,
        scratch_shapes=[
            tiles(PLANE), tiles(PLANE), tiles(PLANE), tiles(AHEAD), tiles(PLANE), tiles(PLANE),
            pltpu.VMEM((2, BLK, DH), F32),
            dma((2,)), dma((4,)), dma,
            dma, dma((PLANE,)), dma, dma((PLANE,)), dma, dma((PLANE,)), dma, dma((AHEAD,)),
        ],
        compiler_params=pltpu.CompilerParams(
            collective_id=1, has_side_effects=True, vmem_limit_bytes=16 * MIB
        ),
        name="scatter",
    )(in_vmem(att), in_vmem(dq), in_vmem(dkv))
    return pl.pallas_call(
        finish_kernel,
        out_shape=tuple(shape(query.shape, BF16) for _ in range(4)),
        in_specs=[vmem] * 4,
        out_specs=[vmem] * 4,
        compiler_params=pltpu.CompilerParams(vmem_limit_bytes=8 * MIB),
        name="finish",
    )(*[in_vmem(out) for out in outs])


def solution(mesh):
    tm_head = P("tm", "head")
    return jax.shard_map(
        per_device,
        mesh=mesh,
        in_specs=(tm_head, tm_head, tm_head, tm_head, P(), P(), P("head")),
        out_specs=(tm_head, tm_head, tm_head, tm_head),
        check_vma=False,
    )
```
